32 devices in a mesh: parts: 2 (over y), rows: 4 (over z), cols: 2 (over x), rank: 2 (over core).
Axes of the slice: x: 2, y: 2, z: 4, core: 2. Of those that a mesh axis runs over, the one named last changes fastest.
Arguments:
- probes: bfloat16 [32768, 128], P(('parts', 'rows', 'cols')), parts along dimension 0, may hold values from -6 to 6
- basis_one: bfloat16 [32768, 256], P(('parts', 'rows', 'cols'), 'rank'), parts along dimension 0, may hold values from -0.375 to 0.375
- basis_two: bfloat16 [32768, 256], P(('parts', 'rows', 'cols'), 'rank'), parts along dimension 0, may hold values from -0.375 to 0.375
- basis_three: bfloat16 [32768, 256], P(('parts', 'rows', 'cols'), 'rank'), parts along dimension 0, may hold values from -0.375 to 0.375
- coeff_one: bfloat16 [32768, 256], P(('parts', 'rows', 'cols'), 'rank'), parts along dimension 0, may hold values from -0.0625 to 0.0625
- coeff_two: bfloat16 [32768, 256], P(('parts', 'rows', 'cols'), 'rank'), parts along dimension 0, may hold values from -0.09375 to 0.09375
- coeff_three: bfloat16 [32768, 256], P(('parts', 'rows', 'cols'), 'rank'), parts along dimension 0, may hold values from -0.125 to 0.125
- leaves: bfloat16 [128, 256, 256], P(('parts', 'rows', 'cols', 'rank')), parts along dimension 0, may hold values from -0.375 to 0.375
Outputs:
- covariance_power: bfloat16 [32768, 128], P(('parts', 'rows', 'cols', 'rank')), parts along dimension 0
The draws below stay inside these ranges and needn't reach their ends.
There are 2 independent parts, one for each index of `parts`. The reference program is written for one: setup_inputs(seed, part) draws one part's arguments, and reference() takes and returns one part's arrays. A program takes and returns all parts, laid end to end along the dimension named above; each array names one. Nothing has to cross between parts.
All inputs are finite; a program needn't handle non-finite values.
Results may differ from the reference program's by a relative error of at most 0.017.
Values may be sent and summed in bfloat16 or wider, within the bound.
No kernel may reach another device: no remote copies, remote signals or barrier semaphores. Data moves between devices by JAX's collectives and lax.ppermute only.
A program may use at most 64 MiB of HBM per device.

```python
import jax
import jax.numpy as jnp
from jax import lax

K = 256
C = 128
LEAF = 256
PASSES = 2
NPTS = 16384


def block_scale(rng, dims, cuts, low, high):
    loudness = 1.0
    for dim, blocks in cuts:
        steps = jax.random.uniform(jax.random.fold_in(jax.random.fold_in(rng, 6), dim), (blocks,), jnp.float32, low / len(cuts), high / len(cuts))
        loudness = loudness * jnp.repeat(jnp.exp(steps), dims[dim] // blocks).reshape((-1,) + (1,) * (len(dims) - 1 - dim))
    return loudness


def scatter_about(key, dims, width, reach, split=(), kind=jnp.bfloat16):
    drawn = width * jax.random.normal(key, dims, jnp.float32)
    if split:
        drawn = drawn * block_scale(key, dims, split, -0.22, 0.18)
    return jnp.clip(drawn, -reach, reach).astype(kind)


def setup_inputs(seed: int = 0, part: int = 0) -> dict:
    keys = jax.random.split(jax.random.key(seed), 9)
    own_keys = jax.random.split(jax.random.fold_in(keys[8], part), 9)
    return {
        "probes": scatter_about(own_keys[0], (NPTS, C), 1.0, 6.0, ((0, 8),)),
        "basis_one": scatter_about(own_keys[1], (NPTS, K), K ** -0.5, 0.375, ((0, 8), (1, 2))),
        "basis_two": scatter_about(own_keys[2], (NPTS, K), K ** -0.5, 0.375, ((0, 8), (1, 2))),
        "basis_three": scatter_about(own_keys[3], (NPTS, K), K ** -0.5, 0.375, ((0, 8), (1, 2))),
        "coeff_one": scatter_about(own_keys[4], (NPTS, K), (NPTS // 2) ** -0.5, 0.0625, ((0, 8), (1, 2))),
        "coeff_two": scatter_about(own_keys[5], (NPTS, K), (NPTS // 4) ** -0.5, 0.09375, ((0, 8), (1, 2))),
        "coeff_three": scatter_about(own_keys[6], (NPTS, K), (NPTS // 8) ** -0.5, 0.125, ((0, 8), (1, 2))),
        "leaves": scatter_about(own_keys[7], (NPTS // LEAF, LEAF, LEAF), LEAF ** -0.5, 0.375, ((0, 16),)),
    }


def apply_once(current, outside, inside, leaves, flipped):
    values = current.astype(jnp.float32)
    summed = jnp.zeros((NPTS, C), jnp.float32)
    for level_index in range(3):
        blocks = 2 ** (level_index + 1)
        former = inside[level_index].astype(jnp.float32).reshape(blocks, -1, K)
        pieces = values.reshape(blocks, -1, C)
        projected = jnp.einsum("bnk,bnc->bkc", former, pieces, precision=lax.Precision.HIGHEST).astype(jnp.bfloat16)
        swapped = projected.reshape(blocks // 2, 2, K, C)[:, ::-1].reshape(blocks, K, C).astype(jnp.float32)
        latter = outside[level_index].astype(jnp.float32).reshape(blocks, -1, K)
        summed = summed + jnp.einsum("bnk,bkc->bnc", latter, swapped, precision=lax.Precision.HIGHEST).reshape(NPTS, C)
    dense = leaves.astype(jnp.float32)
    pieces = values.reshape(-1, LEAF, C)
    pattern = "bji,bjc->bic" if flipped else "bij,bjc->bic"
    summed = summed + jnp.einsum(pattern, dense, pieces, precision=lax.Precision.HIGHEST).reshape(NPTS, C)
    return summed.astype(jnp.bfloat16)


def reference(probes, basis_one, basis_two, basis_three, coeff_one, coeff_two, coeff_three, leaves):
    uppers = (basis_one, basis_two, basis_three)
    lowers = (coeff_one, coeff_two, coeff_three)
    current = probes
    for repeat in range(PASSES):
        current = apply_once(current, lowers, uppers, leaves, True)
        current = apply_once(current, uppers, lowers, leaves, False)
    return current
```

```python
import jax
import jax.numpy as jnp
from jax import lax
from jax.sharding import PartitionSpec as P

LEAF = 256
PASSES = 2
BF = jnp.bfloat16
F32 = jnp.float32


def over_chips(value, stride):
    axes = ("rows", "cols")
    mask = 2**stride
    return lax.ppermute(value, axes, [(s, s ^ mask) for s in range(lax.axis_size(axes))])


def over_rank(value):
    n = lax.axis_size("rank")
    return lax.ppermute(value, "rank", [(s, (s + 1) % n) for s in range(n)])


def siblings_of(partials):
    bits = lax.axis_size(("rows", "cols")).bit_length() - 1
    depth = len(partials)
    k = partials[0].shape[0]
    found = [None] * depth
    live = list(partials)
    for bit in range(bits):
        count = min(depth, bits - bit)
        received = over_chips(jnp.concatenate(live[:count], 0), bit)
        for level in range(count):
            piece = received[level * k : (level + 1) * k]
            if bit == bits - 1 - level:
                found[level] = piece
            else:
                live[level] = (live[level].astype(F32) + piece.astype(F32)).astype(BF)
    return found


def local(probes, basis_one, basis_two, basis_three, coeff_one, coeff_two, coeff_three, leaves):
    place = lax.axis_index("rank")
    rows, cols = probes.shape
    half = rows // lax.axis_size("rank")
    uppers = (basis_one, basis_two, basis_three)
    lowers = (coeff_one, coeff_two, coeff_three)
    other = over_rank(leaves)
    dense = jnp.where(place == 0, jnp.concatenate([leaves, other], 0), jnp.concatenate([other, leaves], 0))
    field = probes
    applies = 2 * PASSES
    for step in range(applies):
        flipped = step % 2 == 0
        outside, inside = (lowers, uppers) if flipped else (uppers, lowers)
        partials = [
            jnp.einsum("nk,nc->kc", factor, field, preferred_element_type=F32).astype(BF) for factor in inside
        ]
        siblings = siblings_of(partials)
        pattern = "bji,bjc->bic" if flipped else "bij,bjc->bic"
        last = step + 1 == applies
        if last:
            mine = lax.dynamic_slice_in_dim(field, place * half, half, 0)
            blocks = leaves
        else:
            mine, blocks = field, dense
        leaf_term = jnp.einsum(
            pattern, blocks, mine.reshape(-1, LEAF, cols), preferred_element_type=F32
        ).reshape(-1, cols)
        term = jnp.dot(outside[0], siblings[0], preferred_element_type=F32)
        for factor, sibling in zip(outside[1:], siblings[1:]):
            term = term + jnp.dot(factor, sibling, preferred_element_type=F32)
        term = term.astype(BF)
        if last:
            keep = lax.dynamic_slice_in_dim(term, place * half, half, 0)
            send = lax.dynamic_slice_in_dim(term, (1 - place) * half, half, 0)
        else:
            keep = send = term
        field = (keep.astype(F32) + over_rank(send).astype(F32) + leaf_term).astype(BF)
    return field


def solution(mesh):
    rows = P(("parts", "rows", "cols"), None)
    split = P(("parts", "rows", "cols"), "rank")
    every = ("parts", "rows", "cols", "rank")
    in_specs = (rows,) + (split,) * 6 + (P(every, None, None),)
    return jax.shard_map(local, mesh=mesh, in_specs=in_specs, out_specs=P(every, None), check_vma=False)
```

```python
import jax
import jax.numpy as jnp
from jax import lax
from jax.experimental import pallas as pl
from jax.experimental.pallas import tpu as pltpu
from jax.sharding import PartitionSpec as P

PASSES = 2
LEVELS = 3
BF = jnp.bfloat16
F32 = jnp.float32
VMEM_BYTES = 12 * 2**20


def mm(a, b, ca, cb):
    return lax.dot_general(a, b, (((ca,), (cb,)), ((), ())), preferred_element_type=F32)


def call(kernel, outs, args, flops, scratch=()):
    vm = pl.BlockSpec(memory_space=pltpu.VMEM)
    moved = sum(a.size * a.dtype.itemsize for a in args[1:]) + sum(o.size * o.dtype.itemsize for o in outs)
    return pl.pallas_call(
        kernel,
        out_shape=outs,
        in_specs=[pl.BlockSpec(memory_space=pltpu.SMEM)] + [vm] * (len(args) - 1),
        out_specs=[vm] * len(outs),
        scratch_shapes=list(scratch),
        cost_estimate=pl.CostEstimate(flops=flops, bytes_accessed=moved, transcendentals=0),
        compiler_params=pltpu.CompilerParams(vmem_limit_bytes=VMEM_BYTES),
    )(*args)


def at(start, size):
    return pl.ds(pl.multiple_of(start, size), size)


def first_kernel(place, z, *refs):
    factors, out = refs[:LEVELS], refs[LEVELS]
    zt = z[...].T
    c = zt.shape[0]
    for level, factor in enumerate(factors):
        out[level * c : (level + 1) * c, :] = mm(zt, factor[...], 1, 0).astype(BF)


def gram_kernel(place, *refs):
    own, (other, full, gram) = refs[:LEVELS], refs[LEVELS:]
    half, k = other.shape[0] // LEVELS, other.shape[1]
    me = place[0]
    for level in range(LEVELS):
        full[:, at((2 * level + me) * k, k)] = own[level][at(me * half, half), :]
        full[:, at((2 * level + 1 - me) * k, k)] = other[level * half : (level + 1) * half, :]
    for i in range(LEVELS):
        rows = slice(2 * k * i, 2 * k * (i + 1))
        left = full[:, rows].T
        for j in range(i + 1):
            cols = slice(2 * k * j, 2 * k * (j + 1))
            block = mm(left, full[:, cols], 1, 0).astype(BF)
            gram[rows, cols] = block
            if j < i:
                gram[cols, rows] = block.T


def join(place, own, other, joined):
    c, k = own.shape[0] // LEVELS, own.shape[1]
    me = place[0]
    for level in range(LEVELS):
        joined[:, at((2 * level + me) * k, k)] = own[level * c : (level + 1) * c, :]
        joined[:, at((2 * level + 1 - me) * k, k)] = other[level * c : (level + 1) * c, :]


def next_kernel(place, own, other, gram, here, there, out, joined):
    join(place, own, other, joined)
    c, k = own.shape[0] // LEVELS, own.shape[1]
    me = place[0]
    q = joined[...]
    for level in range(LEVELS):
        cols = at((2 * level + me) * k, k)
        base = here[:, cols].astype(F32) + there[:, cols].astype(F32)
        out[level * c : (level + 1) * c, :] = (mm(q, gram[:, cols], 1, 0) + base).astype(BF)


def leaf_terms(z, leaves, flipped, out):
    size = leaves.shape[1]
    for q in range(leaves.shape[0]):
        rows = slice(q * size, (q + 1) * size)
        out[rows, :] = mm(leaves[q], z[rows, :], 0 if flipped else 1, 0)


def start_kernel(place, z, leaves, after, y, s):
    half = y.shape[0]
    leaf_terms(z[at(place[0] * half, half), :], leaves, True, y)
    s[...] = mm(y[...].astype(BF).T, after[...], 1, 0).astype(BF)


def field_kernel(flipped, place, q, factor, was, leaves, after, y, s):
    z = (mm(factor[...], q[...], 1, 1) + was[...]).astype(BF)
    leaf_terms(z, leaves, flipped, y)
    s[...] = mm(y[...].astype(BF).T, after[...], 1, 0).astype(BF)


def late_kernel(flipped, place, q, factor, was, leaves, y):
    z = (mm(factor[...], q[...], 1, 1) + was[...]).astype(BF)
    leaf_terms(z, leaves, flipped, y)


def last_kernel(place, own, other, factor, was, out, joined):
    join(place, own, other, joined)
    out[...] = (mm(factor[...], joined[...], 1, 1) + was[...]).astype(BF)


def over_chips(value, stride):
    axes = ("rows", "cols")
    mask = 2**stride
    return lax.ppermute(value, axes, [(s, s ^ mask) for s in range(lax.axis_size(axes))])


def over_rank(value):
    return lax.ppermute(value, "rank", [(0, 1), (1, 0)])


def siblings_of(packed):
    bits = lax.axis_size(("rows", "cols")).bit_length() - 1
    c = packed.shape[0] // LEVELS
    found = [None] * LEVELS
    for bit in range(bits):
        received = over_chips(packed, bit)
        count = min(LEVELS, bits - bit)
        if bit == bits - count:
            found[count - 1] = received[(count - 1) * c :]
            count -= 1
            packed, received = packed[: count * c], received[: count * c]
        packed = (packed.astype(F32) + received.astype(F32)).astype(BF)
    return found


def local(probes, basis_one, basis_two, basis_three, coeff_one, coeff_two, coeff_three, leaves):
    rank = lax.axis_index("rank")
    place = rank.reshape(1)
    n, c = probes.shape
    half = n // 2
    k = basis_one.shape[1]
    wide = 2 * k * LEVELS
    S = jax.ShapeDtypeStruct
    uppers = (basis_one, basis_two, basis_three)
    lowers = (coeff_one, coeff_two, coeff_three)

    def swapped(factors):
        return over_rank(
            jnp.concatenate([lax.dynamic_slice_in_dim(f, (1 - rank) * half, half, 0) for f in factors], 0)
        )

    def prepared(factors, other):
        full, gram = call(
            gram_kernel, [S((half, wide), BF), S((wide, wide), BF)], (place, *factors, other), half * wide * wide * 3 // 2
        )
        return full, (gram.astype(F32) + over_rank(gram).astype(F32)).astype(BF)

    (packed,) = call(first_kernel, [S((LEVELS * c, k), BF)], (place, probes, *uppers), 2 * n * LEVELS * k * c)
    lower, lower_gram = prepared(lowers, swapped(lowers))
    upper, upper_gram = prepared(uppers, swapped(uppers))
    y_shape, s_shape = S((half, c), F32), S((c, wide), BF)
    field_flops = 4 * half * wide * c
    y, s = call(start_kernel, [y_shape, s_shape], (place, probes, leaves, lower), field_flops // 2)
    applies = 2 * PASSES
    for step in range(applies):
        flipped = step % 2 == 0
        factor, gram, after = (lower, lower_gram, upper) if flipped else (upper, upper_gram, lower)
        found = siblings_of(packed)
        own = jnp.concatenate(found, 0)
        other = over_rank(own)
        joined = pltpu.VMEM((c, wide), BF)
        if step + 1 == applies:
            (out,) = call(last_kernel, [S((half, c), BF)], (place, own, other, factor, y), field_flops // 2, [joined])
            return out
        packed, q = call(
            next_kernel,
            [S((LEVELS * c, k), BF), s_shape],
            (place, own, other, gram, s, over_rank(s)),
            wide * wide * c,
        )
        if step + 2 == applies:
            (y,) = call(lambda *r: late_kernel(not flipped, *r), [y_shape], (place, q, factor, y, leaves), field_flops // 2)
        else:
            y, s = call(
                lambda *r: field_kernel(not flipped, *r), [y_shape, s_shape], (place, q, factor, y, leaves, after), field_flops
            )


def solution(mesh):
    rows = P(("parts", "rows", "cols"), None)
    split = P(("parts", "rows", "cols"), "rank")
    every = ("parts", "rows", "cols", "rank")
    in_specs = (rows,) + (split,) * 6 + (P(every, None, None),)
    return jax.shard_map(local, mesh=mesh, in_specs=in_specs, out_specs=P(every, None), check_vma=False)
```

```python
import jax
import jax.numpy as jnp
from jax import lax
from jax.experimental import pallas as pl
from jax.experimental.pallas import tpu as pltpu
from jax.sharding import PartitionSpec as P

PASSES = 2
LEVELS = 3
BF = jnp.bfloat16
F32 = jnp.float32
VMEM_BYTES = 12 * 2**20


def mm(a, b, ca, cb):
    return lax.dot_general(a, b, (((ca,), (cb,)), ((), ())), preferred_element_type=F32)


def call(kernel, outs, args, flops, scratch=()):
    vm = pl.BlockSpec(memory_space=pltpu.VMEM)
    moved = sum(a.size * a.dtype.itemsize for a in args[1:]) + sum(o.size * o.dtype.itemsize for o in outs)
    return pl.pallas_call(
        kernel,
        out_shape=outs,
        in_specs=[pl.BlockSpec(memory_space=pltpu.SMEM)] + [vm] * (len(args) - 1),
        out_specs=[vm] * len(outs),
        scratch_shapes=list(scratch),
        cost_estimate=pl.CostEstimate(flops=flops, bytes_accessed=moved, transcendentals=0),
        compiler_params=pltpu.CompilerParams(vmem_limit_bytes=VMEM_BYTES),
    )(*args)


def at(start, size):
    return pl.ds(pl.multiple_of(start, size), size)


def first_kernel(place, z, *refs):
    factors, out = refs[:LEVELS], refs[LEVELS]
    zt = z[...].T
    c = zt.shape[0]
    for level, factor in enumerate(factors):
        out[level * c : (level + 1) * c, :] = mm(zt, factor[...], 1, 0).astype(BF)


def join_kernel(place, own, other, out):
    k = own.shape[1]
    me = place[0]
    out[:, at(me * k, k)] = own[...]
    out[:, at((1 - me) * k, k)] = other[...]


def gram_kernel(place, *refs):
    own, (other, full, gram) = refs[:LEVELS], refs[LEVELS:]
    half, k = other.shape[0] // LEVELS, other.shape[1]
    me = place[0]
    for level in range(LEVELS):
        full[:, at((2 * level + me) * k, k)] = own[level][at(me * half, half), :]
        full[:, at((2 * level + 1 - me) * k, k)] = other[level * half : (level + 1) * half, :]
    for i in range(LEVELS):
        rows = slice(2 * k * i, 2 * k * (i + 1))
        left = full[:, rows].T
        for j in range(i + 1):
            cols = slice(2 * k * j, 2 * k * (j + 1))
            block = mm(left, full[:, cols], 1, 0).astype(BF)
            gram[rows, cols] = block
            if j < i:
                gram[cols, rows] = block.T


def next_kernel(place, *refs):
    found, (gram, here, there, out) = refs[:LEVELS], refs[LEVELS:]
    c, k = found[0].shape
    for level in range(LEVELS):
        cols = slice(level * k, (level + 1) * k)
        total = here[:, cols].astype(F32) + there[:, cols].astype(F32)
        for i, q in enumerate(found):
            total = total + mm(q[...], gram[i * k : (i + 1) * k, cols], 1, 0)
        out[level * c : (level + 1) * c, :] = total.astype(BF)


def chosen(place, holders, refs, joined):
    k = refs[0].shape[1]
    for level, holder in enumerate(holders):
        received, relayed = refs[2 * level], refs[2 * level + 1]
        cols = slice(level * k, (level + 1) * k)

        @pl.when(place[0] == holder)
        def _():
            joined[:, cols] = received[...]

        @pl.when(place[0] != holder)
        def _():
            joined[:, cols] = relayed[...]


def again_kernel(holders, place, *refs):
    pieces, (gram, here, there, out, joined) = refs[: 2 * LEVELS], refs[2 * LEVELS :]
    chosen(place, holders, pieces, joined)
    c, k = pieces[0].shape
    for level in range(LEVELS):
        cols = slice(level * k, (level + 1) * k)
        total = here[:, cols].astype(F32) + there[:, cols].astype(F32) + mm(joined[...], gram[:, cols], 1, 0)
        out[level * c : (level + 1) * c, :] = total.astype(BF)


def leaf_terms(z, leaves, flipped, out):
    size = leaves.shape[1]
    for q in range(leaves.shape[0]):
        rows = slice(q * size, (q + 1) * size)
        out[rows, :] = mm(leaves[q], z[rows, :], 0 if flipped else 1, 0)


def start_kernel(place, z, leaves, after, y, s):
    half = y.shape[0]
    leaf_terms(z[at(place[0] * half, half), :], leaves, True, y)
    s[...] = mm(y[...].astype(BF).T, after[...], 1, 0).astype(BF)


def field_kernel(flipped, place, q, factor, was, leaves, after, y, s):
    z = (mm(factor[...], q[...], 1, 1) + was[...]).astype(BF)
    leaf_terms(z, leaves, flipped, y)
    s[...] = mm(y[...].astype(BF).T, after[...], 1, 0).astype(BF)


def late_kernel(flipped, place, q, factor, was, leaves, y):
    z = (mm(factor[...], q[...], 1, 1) + was[...]).astype(BF)
    leaf_terms(z, leaves, flipped, y)


def last_kernel(holders, place, *refs):
    pieces, (factor, was, out, joined) = refs[: 2 * LEVELS], refs[2 * LEVELS :]
    chosen(place, holders, pieces, joined)
    out[...] = (mm(factor[...], joined[...], 1, 1) + was[...]).astype(BF)


def one_way(value, stride, source):
    mask = 2**stride
    chips = lax.axis_size(("rows", "cols"))
    away = [(2 * p + source, 2 * (p ^ mask) + 1 - source) for p in range(chips)]
    home = [(2 * p + 1 - source, 2 * p + source) for p in range(chips)]
    return lax.ppermute(value, ("rows", "cols", "rank"), away + home)


def over_rank(value):
    return lax.ppermute(value, "rank", [(0, 1), (1, 0)])


def add(a, b):
    return (a.astype(F32) + b.astype(F32)).astype(BF)


def siblings_of(packed, summed, source):
    rank = lax.axis_index("rank")
    bits = lax.axis_size(("rows", "cols")).bit_length() - 1
    c = packed.shape[0] // LEVELS
    found = [None] * LEVELS
    for bit in range(bits):
        count = min(LEVELS, bits - bit)
        received = one_way(packed[: count * c], bit, source)
        done = bit == bits - count
        onward = min(LEVELS, max(bits - bit - 2, 0))
        relay = [l for l in range(count) if l < onward or (done and l == count - 1)]
        if relay:
            sent = jnp.concatenate([received[l * c : (l + 1) * c] for l in relay], 0)
            relayed = over_rank(sent)
        if done:
            found[count - 1] = (received[(count - 1) * c :], relayed[(len(relay) - 1) * c :], 1 - source)
            count -= 1
        packed = add(summed[: count * c], received[: count * c])
        if onward:
            got = jnp.where(rank == source, relayed[: onward * c], received[: onward * c])
            summed = add(summed[: onward * c], got)
        source = 1 - source
    return found, source


def local(probes, basis_one, basis_two, basis_three, coeff_one, coeff_two, coeff_three, leaves):
    rank = lax.axis_index("rank")
    place = rank.reshape(1)
    n, c = probes.shape
    half = n // 2
    k = basis_one.shape[1]
    wide = 2 * k * LEVELS
    S = jax.ShapeDtypeStruct
    p_shape, y_shape, s_shape = S((LEVELS * c, 2 * k), BF), S((half, c), F32), S((c, wide), BF)
    uppers = (basis_one, basis_two, basis_three)
    lowers = (coeff_one, coeff_two, coeff_three)

    def swapped(factors):
        return over_rank(
            jnp.concatenate([lax.dynamic_slice_in_dim(f, (1 - rank) * half, half, 0) for f in factors], 0)
        )

    def prepared(factors, other):
        full, gram = call(
            gram_kernel, [S((half, wide), BF), S((wide, wide), BF)], (place, *factors, other), half * wide * wide * 3 // 2
        )
        return full, add(gram, over_rank(gram))

    (own,) = call(first_kernel, [S((LEVELS * c, k), BF)], (place, probes, *uppers), 2 * n * LEVELS * k * c)
    own, lowers, uppers = lax.optimization_barrier((own, lowers, uppers))
    (packed,) = call(join_kernel, [p_shape], (place, own, over_rank(own)), 0)
    summed = packed
    lower, lower_gram = prepared(lowers, swapped(lowers))
    upper, upper_gram = prepared(uppers, swapped(uppers))
    field_flops = 4 * half * wide * c
    y, s = call(start_kernel, [y_shape, s_shape], (place, probes, leaves, lower), field_flops // 2)
    applies = 2 * PASSES
    source = 0
    joined = pltpu.VMEM((c, wide), BF)
    for step in range(applies):
        flipped = step % 2 == 0
        factor, gram, after = (lower, lower_gram, upper) if flipped else (upper, upper_gram, lower)
        found, source = siblings_of(packed, summed, source)
        holders = [f[2] for f in found]
        pieces = [x for f in found for x in f[:2]]
        if step + 1 == applies:
            (out,) = call(
                lambda *r: last_kernel(holders, *r), [S((half, c), BF)], (place, *pieces, factor, y), field_flops // 2, [joined]
            )
            return out
        there = over_rank(s)
        early = [f[0] if f[2] == source else f[1] for f in found]
        (packed,) = call(next_kernel, [p_shape], (place, *early, gram, s, there), 2 * wide * wide * c)
        summed, q = call(
            lambda *r: again_kernel(holders, *r), [p_shape, s_shape], (place, *pieces, gram, s, there), 2 * wide * wide * c
        )
        if step + 2 == applies:
            (y,) = call(lambda *r: late_kernel(not flipped, *r), [y_shape], (place, q, factor, y, leaves), field_flops // 2)
        else:
            y, s = call(
                lambda *r: field_kernel(not flipped, *r),
                [y_shape, s_shape],
                (place, q, factor, y, leaves, after),
                field_flops,
            )


def solution(mesh):
    rows = P(("parts", "rows", "cols"), None)
    split = P(("parts", "rows", "cols"), "rank")
    every = ("parts", "rows", "cols", "rank")
    in_specs = (rows,) + (split,) * 6 + (P(every, None, None),)
    return jax.shard_map(local, mesh=mesh, in_specs=in_specs, out_specs=P(every, None), check_vma=False)
```

```python
import jax
import jax.numpy as jnp
from jax import lax
from jax.experimental import pallas as pl
from jax.experimental.pallas import tpu as pltpu
from jax.sharding import PartitionSpec as P


PASSES = 2
LEVELS = 3
BF = jnp.bfloat16
F32 = jnp.float32
VMEM_BYTES = 12 * 2**20


def mm(a, b, ca, cb):
    return lax.dot_general(a, b, (((ca,), (cb,)), ((), ())), preferred_element_type=F32)


def call(kernel, outs, args, flops, scratch=(), far=0, room=VMEM_BYTES):
    vm = pl.BlockSpec(memory_space=pltpu.VMEM)
    hbm = pl.BlockSpec(memory_space=pltpu.HBM)
    moved = sum(a.size * a.dtype.itemsize for a in args[1:]) + sum(o.size * o.dtype.itemsize for o in outs)
    return pl.pallas_call(
        kernel,
        out_shape=outs,
        in_specs=[pl.BlockSpec(memory_space=pltpu.SMEM)] + [vm] * (len(args) - 1 - far) + [hbm] * far,
        out_specs=[vm] * len(outs),
        scratch_shapes=list(scratch),
        cost_estimate=pl.CostEstimate(flops=flops, bytes_accessed=moved, transcendentals=0),
        compiler_params=pltpu.CompilerParams(vmem_limit_bytes=room),
    )(*args)


def at(start, size):
    return pl.ds(pl.multiple_of(start, size), size)


def first_kernel(place, *refs):
    sources, out, buffers, sems = refs[: LEVELS + 1], refs[LEVELS + 1], refs[LEVELS + 2 : -1], refs[-1]
    copies = [pltpu.make_async_copy(a, b, sems.at[i]) for i, (a, b) in enumerate(zip(sources, buffers))]
    for copy in copies:
        copy.start()
    copies[0].wait()
    zt = buffers[0][...].T
    c = zt.shape[0]
    for level in range(LEVELS):
        copies[1 + level].wait()
        out[level * c : (level + 1) * c, :] = mm(zt, buffers[1 + level][...], 1, 0).astype(BF)


def pack_kernel(place, *refs):
    sources, out, sems = refs[:LEVELS], refs[LEVELS], refs[LEVELS + 1]
    half = out.shape[0] // LEVELS
    copies = [
        pltpu.make_async_copy(a.at[at((1 - place[0]) * half, half), :], out.at[pl.ds(i * half, half), :], sems.at[i])
        for i, a in enumerate(sources)
    ]
    for copy in copies:
        copy.start()
    for copy in copies:
        copy.wait()


def join_kernel(place, own, other, out):
    k = own.shape[1]
    me = place[0]
    out[:, at(me * k, k)] = own[...]
    out[:, at((1 - me) * k, k)] = other[...]


def gram_kernel(place, other, *refs):
    own, (full, gram, sems) = refs[:LEVELS], refs[LEVELS:]
    half, k = other.shape[0] // LEVELS, other.shape[1]
    me = place[0]
    copies = [
        pltpu.make_async_copy(a.at[at(me * half, half), :], full.at[:, at((2 * i + me) * k, k)], sems.at[i])
        for i, a in enumerate(own)
    ]
    for copy in copies:
        copy.start()
    for level in range(LEVELS):
        full[:, at((2 * level + 1 - me) * k, k)] = other[level * half : (level + 1) * half, :]
    for copy in copies:
        copy.wait()
    for i in range(LEVELS):
        rows = slice(2 * k * i, 2 * k * (i + 1))
        left = full[:, rows].T
        for j in range(i + 1):
            cols = slice(2 * k * j, 2 * k * (j + 1))
            block = mm(left, full[:, cols], 1, 0).astype(BF)
            gram[rows, cols] = block
            if j < i:
                gram[cols, rows] = block.T


def next_kernel(place, *refs):
    found, (gram, here, there, out) = refs[:LEVELS], refs[LEVELS:]
    c, k = found[0].shape
    for level in range(LEVELS):
        cols = slice(level * k, (level + 1) * k)
        total = here[:, cols].astype(F32) + there[:, cols].astype(F32)
        for i, q in enumerate(found):
            total = total + mm(q[...], gram[i * k : (i + 1) * k, cols], 1, 0)
        out[level * c : (level + 1) * c, :] = total.astype(BF)


def chosen(place, holders, refs, joined):
    k = refs[0].shape[1]
    for level, holder in enumerate(holders):
        received, relayed = refs[2 * level], refs[2 * level + 1]
        cols = slice(level * k, (level + 1) * k)

        @pl.when(place[0] == holder)
        def _():
            joined[:, cols] = received[...]

        @pl.when(place[0] != holder)
        def _():
            joined[:, cols] = relayed[...]


def again_kernel(holders, place, *refs):
    pieces, (gram, here, there, out, joined) = refs[: 2 * LEVELS], refs[2 * LEVELS :]
    chosen(place, holders, pieces, joined)
    c, k = pieces[0].shape
    for level in range(LEVELS):
        cols = slice(level * k, (level + 1) * k)
        total = here[:, cols].astype(F32) + there[:, cols].astype(F32) + mm(joined[...], gram[:, cols], 1, 0)
        out[level * c : (level + 1) * c, :] = total.astype(BF)


def sum_kernel(source, place, summed, received, relayed, out):
    n = out.shape[0]

    @pl.when(place[0] == source)
    def _():
        out[...] = add(summed[:n, :], relayed[:n, :])

    @pl.when(place[0] != source)
    def _():
        out[...] = add(summed[:n, :], received[:n, :])


def leaf_terms(z, leaves, flipped, out):
    size = leaves.shape[1]
    for q in range(leaves.shape[0]):
        rows = slice(q * size, (q + 1) * size)
        out[rows, :] = mm(leaves[q], z[rows, :], 0 if flipped else 1, 0)


def start_kernel(place, z, leaves, after, y, s):
    half = y.shape[0]
    leaf_terms(z[at(place[0] * half, half), :], leaves, True, y)
    s[...] = mm(y[...].astype(BF).T, after[...], 1, 0).astype(BF)


def field_kernel(flipped, place, q, factor, was, leaves, after, y, s):
    z = (mm(factor[...], q[...], 1, 1) + was[...]).astype(BF)
    leaf_terms(z, leaves, flipped, y)
    s[...] = mm(y[...].astype(BF).T, after[...], 1, 0).astype(BF)


def late_kernel(flipped, place, q, factor, was, leaves, y):
    z = (mm(factor[...], q[...], 1, 1) + was[...]).astype(BF)
    leaf_terms(z, leaves, flipped, y)


def most_kernel(holders, place, *refs):
    pieces, (factor, was, y, joined) = refs[: 2 * LEVELS - 2], refs[2 * LEVELS - 2 :]
    chosen(place, holders, pieces, joined)
    y[...] = mm(factor[:, pieces[0].shape[1] :], joined[...], 1, 1) + was[...]


def last_kernel(holders, place, received, relayed, factor, was, out, joined):
    chosen(place, holders, (received, relayed), joined)
    out[...] = (mm(factor[:, : received.shape[1]], joined[...], 1, 1) + was[...]).astype(BF)


def one_way(value, stride, source):
    mask = 2**stride
    chips = lax.axis_size(("rows", "cols"))
    away = [(2 * p + source, 2 * (p ^ mask) + 1 - source) for p in range(chips)]
    home = [(2 * p + 1 - source, 2 * p + source) for p in range(chips)]
    return lax.ppermute(value, ("rows", "cols", "rank"), away + home)


def over_rank(value):
    return lax.ppermute(value, "rank", [(0, 1), (1, 0)])


def add(a, b):
    return (a.astype(F32) + b.astype(F32)).astype(BF)


def siblings_of(place, packed, summed, source):
    bits = lax.axis_size(("rows", "cols")).bit_length() - 1
    c = packed.shape[0] // LEVELS
    found = [None] * LEVELS
    for bit in range(bits):
        count = min(LEVELS, bits - bit)
        received = one_way(packed[: count * c], bit, source)
        done = bit == bits - count
        onward = min(LEVELS, max(bits - bit - 2, 0))
        relay = [l for l in range(count) if l < onward or (done and l == count - 1)]
        if relay:
            sent = jnp.concatenate([received[l * c : (l + 1) * c] for l in relay], 0)
            relayed = over_rank(sent)
        if done:
            found[count - 1] = (received[(count - 1) * c :], relayed[(len(relay) - 1) * c :], 1 - source)
            count -= 1
        packed = add(summed[: count * c], received[: count * c])
        if onward:
            shape = jax.ShapeDtypeStruct((onward * c, packed.shape[1]), BF)
            (summed,) = call(
                lambda *r, source=source: sum_kernel(source, *r), [shape], (place, summed, received, relayed), 0
            )
        source = 1 - source
    return found, source


def local(probes, basis_one, basis_two, basis_three, coeff_one, coeff_two, coeff_three, leaves):
    place = lax.axis_index("rank").reshape(1)
    n, c = probes.shape
    half = n // 2
    k = basis_one.shape[1]
    wide = 2 * k * LEVELS
    S = jax.ShapeDtypeStruct
    p_shape, y_shape, s_shape = S((LEVELS * c, 2 * k), BF), S((half, c), F32), S((c, wide), BF)
    sems = pltpu.SemaphoreType.DMA
    uppers = (basis_one, basis_two, basis_three)
    lowers = (coeff_one, coeff_two, coeff_three)

    def prepared(factors):
        (sent,) = call(pack_kernel, [S((LEVELS * half, k), BF)], (place, *factors), 0, [sems((LEVELS,))], LEVELS)
        full, gram = call(
            gram_kernel,
            [S((half, wide), BF), S((wide, wide), BF)],
            (place, over_rank(sent), *factors),
            half * wide * wide * 3 // 2,
            [sems((LEVELS,))],
            LEVELS,
        )
        return full, add(gram, over_rank(gram))

    buffers = [pltpu.VMEM(a.shape, BF) for a in (probes, *uppers)]
    (own,) = call(
        first_kernel,
        [S((LEVELS * c, k), BF)],
        (place, probes, *uppers),
        2 * n * LEVELS * k * c,
        [*buffers, sems((LEVELS + 1,))],
        LEVELS + 1,
        None,
    )
    (packed,) = call(join_kernel, [p_shape], (place, own, over_rank(own)), 0)
    packed, lowers, probes, leaves = lax.optimization_barrier((packed, lowers, probes, leaves))
    summed = packed
    lower, lower_gram = prepared(lowers)
    field_flops = 4 * half * wide * c
    y, s = call(start_kernel, [y_shape, s_shape], (place, probes, leaves, lower), field_flops // 2)
    applies = 2 * PASSES
    source = 0
    for step in range(applies):
        flipped = step % 2 == 0
        found, source = siblings_of(place, packed, summed, source)
        holders = [f[2] for f in found]
        pieces = [x for f in found for x in f[:2]]
        if step + 1 == applies:
            rest = pltpu.VMEM((c, wide - 2 * k), BF)
            (y,) = call(
                lambda *r: most_kernel(holders[1:], *r), [y_shape], (place, *pieces[2:], upper, y), field_flops // 3, [rest]
            )
            (out,) = call(
                lambda *r: last_kernel(holders[:1], *r),
                [S((half, c), BF)],
                (place, *pieces[:2], upper, y),
                field_flops // 6,
                [pltpu.VMEM((c, 2 * k), BF)],
            )
            return out
        there = over_rank(s)
        early = [f[0] if f[2] == source else f[1] for f in found]
        gram = lower_gram if flipped else upper_gram
        (packed,) = call(next_kernel, [p_shape], (place, *early, gram, s, there), 2 * wide * wide * c)
        if step == 0:
            packed, uppers = lax.optimization_barrier((packed, uppers))
            upper, upper_gram = prepared(uppers)
        factor, after = (lower, upper) if flipped else (upper, lower)
        summed, q = call(
            lambda *r: again_kernel(holders, *r), [p_shape, s_shape], (place, *pieces, gram, s, there), 2 * wide * wide * c
        )
        if step + 2 == applies:
            (y,) = call(
                lambda *r: late_kernel(not flipped, *r), [y_shape], (place, q, factor, y, leaves), field_flops // 2
            )
        else:
            y, s = call(
                lambda *r: field_kernel(not flipped, *r),
                [y_shape, s_shape],
                (place, q, factor, y, leaves, after),
                field_flops,
            )


def solution(mesh):
    rows = P(("parts", "rows", "cols"), None)
    split = P(("parts", "rows", "cols"), "rank")
    every = ("parts", "rows", "cols", "rank")
    in_specs = (rows,) + (split,) * 6 + (P(every, None, None),)

    return jax.shard_map(local, mesh=mesh, in_specs=in_specs, out_specs=P(every, None), check_vma=False)
```

```python
import jax
import jax.numpy as jnp
from jax import lax
from jax.experimental import pallas as pl
from jax.experimental.pallas import tpu as pltpu
from jax.sharding import PartitionSpec as P


PASSES = 2
LEVELS = 3
CHUNKS = 4
BF = jnp.bfloat16
F32 = jnp.float32
VMEM_BYTES = 12 * 2**20


def mm(a, b, ca, cb):
    return lax.dot_general(a, b, (((ca,), (cb,)), ((), ())), preferred_element_type=F32)


def call(kernel, outs, args, flops, scratch=(), far=0):
    vm = pl.BlockSpec(memory_space=pltpu.VMEM)
    hbm = pl.BlockSpec(memory_space=pltpu.HBM)
    near, distant = args[: len(args) - far], args[len(args) - far :]
    moved = sum(a.size * a.dtype.itemsize for a in args[1:]) + sum(o.size * o.dtype.itemsize for o in outs)
    return pl.pallas_call(
        kernel,
        out_shape=outs,
        in_specs=[pl.BlockSpec(memory_space=pltpu.SMEM)] + [vm] * (len(args) - 1 - far) + [hbm] * far,
        out_specs=[vm] * len(outs),
        scratch_shapes=list(scratch),
        cost_estimate=pl.CostEstimate(flops=flops, bytes_accessed=moved, transcendentals=0),
        compiler_params=pltpu.CompilerParams(vmem_limit_bytes=VMEM_BYTES),
    )(*near, *(pltpu.with_memory_space_constraint(a, pltpu.HBM) for a in distant))


def at(start, size):
    return pl.ds(pl.multiple_of(start, size), size)


def first_kernel(place, *refs):
    sources, out, buffers, sems = refs[: LEVELS + 1], refs[LEVELS + 1], refs[LEVELS + 2 : -1], refs[-1]
    rows = sources[0].shape[0] // CHUNKS
    copies = [
        [
            pltpu.make_async_copy(a.at[pl.ds(j * rows, rows), :], b.at[pl.ds(j * rows, rows), :], sems.at[i, j])
            for j in range(CHUNKS)
        ]
        for i, (a, b) in enumerate(zip(sources, buffers))
    ]
    for group in copies:
        for copy in group:
            copy.start()
    for copy in copies[0]:
        copy.wait()
    zt = buffers[0][...].T
    c = zt.shape[0]
    for level in range(LEVELS):
        for copy in copies[1 + level]:
            copy.wait()
        out[level * c : (level + 1) * c, :] = mm(zt, buffers[1 + level][...], 1, 0).astype(BF)


def pack_kernel(place, *refs):
    sources, out, sems = refs[:LEVELS], refs[LEVELS], refs[LEVELS + 1]
    half = out.shape[0] // LEVELS
    copies = [
        pltpu.make_async_copy(a.at[at((1 - place[0]) * half, half), :], out.at[pl.ds(i * half, half), :], sems.at[i])
        for i, a in enumerate(sources)
    ]
    for copy in copies:
        copy.start()
    for copy in copies:
        copy.wait()


def join_kernel(place, own, other, out):
    k = own.shape[1]
    me = place[0]
    out[:, at(me * k, k)] = own[...]
    out[:, at((1 - me) * k, k)] = other[...]


def gram_kernel(place, other, *refs):
    own, (full, gram, sems) = refs[:LEVELS], refs[LEVELS:]
    half, k = other.shape[0] // LEVELS, other.shape[1]
    me = place[0]
    copies = [
        pltpu.make_async_copy(a.at[at(me * half, half), :], full.at[:, at((2 * i + me) * k, k)], sems.at[i])
        for i, a in enumerate(own)
    ]
    for copy in copies:
        copy.start()
    for level in range(LEVELS):
        full[:, at((2 * level + 1 - me) * k, k)] = other[level * half : (level + 1) * half, :]
    for copy in copies:
        copy.wait()
    for i in range(LEVELS):
        rows = slice(2 * k * i, 2 * k * (i + 1))
        left = full[:, rows].T
        for j in range(i + 1):
            cols = slice(2 * k * j, 2 * k * (j + 1))
            block = mm(left, full[:, cols], 1, 0).astype(BF)
            gram[rows, cols] = block
            if j < i:
                gram[cols, rows] = block.T


def next_kernel(place, *refs):
    found, (gram, here, there, out) = refs[:LEVELS], refs[LEVELS:]
    c, k = found[0].shape
    for level in range(LEVELS):
        cols = slice(level * k, (level + 1) * k)
        total = here[:, cols].astype(F32) + there[:, cols].astype(F32)
        for i, q in enumerate(found):
            total = total + mm(q[...], gram[i * k : (i + 1) * k, cols], 1, 0)
        out[level * c : (level + 1) * c, :] = total.astype(BF)


def chosen(place, holders, refs, joined):
    k = refs[0].shape[1]
    for level, holder in enumerate(holders):
        received, relayed = refs[2 * level], refs[2 * level + 1]
        cols = slice(level * k, (level + 1) * k)

        @pl.when(place[0] == holder)
        def _():
            joined[:, cols] = received[...]

        @pl.when(place[0] != holder)
        def _():
            joined[:, cols] = relayed[...]


def again_kernel(holders, place, *refs):
    pieces, (gram, here, there, out, joined) = refs[: 2 * LEVELS], refs[2 * LEVELS :]
    chosen(place, holders, pieces, joined)
    c, k = pieces[0].shape
    for level in range(LEVELS):
        cols = slice(level * k, (level + 1) * k)
        total = here[:, cols].astype(F32) + there[:, cols].astype(F32) + mm(joined[...], gram[:, cols], 1, 0)
        out[level * c : (level + 1) * c, :] = total.astype(BF)


def sum_kernel(source, place, summed, received, relayed, out):
    n = out.shape[0]

    @pl.when(place[0] == source)
    def _():
        out[...] = add(summed[:n, :], relayed[:n, :])

    @pl.when(place[0] != source)
    def _():
        out[...] = add(summed[:n, :], received[:n, :])


def leaf_terms(z, leaves, flipped, out):
    size = leaves.shape[1]
    for q in range(leaves.shape[0]):
        rows = slice(q * size, (q + 1) * size)
        out[rows, :] = mm(leaves[q], z[rows, :], 0 if flipped else 1, 0)


def start_kernel(place, z, leaves, after, y, s):
    half = y.shape[0]
    leaf_terms(z[at(place[0] * half, half), :], leaves, True, y)
    s[...] = mm(y[...].astype(BF).T, after[...], 1, 0).astype(BF)


def field_kernel(flipped, place, q, factor, was, leaves, after, y, s):
    z = (mm(factor[...], q[...], 1, 1) + was[...]).astype(BF)
    leaf_terms(z, leaves, flipped, y)
    s[...] = mm(y[...].astype(BF).T, after[...], 1, 0).astype(BF)


def late_kernel(flipped, place, q, factor, was, leaves, y):
    z = (mm(factor[...], q[...], 1, 1) + was[...]).astype(BF)
    leaf_terms(z, leaves, flipped, y)


def most_kernel(holders, place, *refs):
    pieces, (factor, was, y, joined) = refs[: 2 * LEVELS - 2], refs[2 * LEVELS - 2 :]
    chosen(place, holders, pieces, joined)
    y[...] = mm(factor[:, pieces[0].shape[1] :], joined[...], 1, 1) + was[...]


def last_kernel(holders, place, received, relayed, factor, was, out, joined):
    chosen(place, holders, (received, relayed), joined)
    out[...] = (mm(factor[:, : received.shape[1]], joined[...], 1, 1) + was[...]).astype(BF)


def one_way(value, stride, source):
    mask = 2**stride
    chips = lax.axis_size(("rows", "cols"))
    away = [(2 * p + source, 2 * (p ^ mask) + 1 - source) for p in range(chips)]
    home = [(2 * p + 1 - source, 2 * p + source) for p in range(chips)]
    return lax.ppermute(value, ("rows", "cols", "rank"), away + home)


def over_rank(value):
    return lax.ppermute(value, "rank", [(0, 1), (1, 0)])


def add(a, b):
    return (a.astype(F32) + b.astype(F32)).astype(BF)


def siblings_of(place, packed, summed, source):
    bits = lax.axis_size(("rows", "cols")).bit_length() - 1
    c = packed.shape[0] // LEVELS
    found = [None] * LEVELS
    for bit in range(bits):
        count = min(LEVELS, bits - bit)
        received = one_way(packed[: count * c], bit, source)
        done = bit == bits - count
        onward = min(LEVELS, max(bits - bit - 2, 0))
        relay = [l for l in range(count) if l < onward or (done and l == count - 1)]
        if relay:
            sent = jnp.concatenate([received[l * c : (l + 1) * c] for l in relay], 0)
            relayed = over_rank(sent)
        if done:
            found[count - 1] = (received[(count - 1) * c :], relayed[(len(relay) - 1) * c :], 1 - source)
            count -= 1
        packed = add(summed[: count * c], received[: count * c])
        if onward:
            shape = jax.ShapeDtypeStruct((onward * c, packed.shape[1]), BF)
            (summed,) = call(
                lambda *r, source=source: sum_kernel(source, *r), [shape], (place, summed, received, relayed), 0
            )
        source = 1 - source
    return found, source


def local(probes, basis_one, basis_two, basis_three, coeff_one, coeff_two, coeff_three, leaves):
    place = lax.axis_index("rank").reshape(1)
    n, c = probes.shape
    half = n // 2
    k = basis_one.shape[1]
    wide = 2 * k * LEVELS
    S = jax.ShapeDtypeStruct
    p_shape, y_shape, s_shape = S((LEVELS * c, 2 * k), BF), S((half, c), F32), S((c, wide), BF)
    sems = pltpu.SemaphoreType.DMA
    uppers = (basis_one, basis_two, basis_three)
    lowers = (coeff_one, coeff_two, coeff_three)

    def prepared(factors):
        (sent,) = call(pack_kernel, [S((LEVELS * half, k), BF)], (place, *factors), 0, [sems((LEVELS,))], LEVELS)
        other = over_rank(sent)
        full, gram = call(
            gram_kernel,
            [S((half, wide), BF), S((wide, wide), BF)],
            (place, other, *factors),
            half * wide * wide * 3 // 2,
            [sems((LEVELS,))],
            LEVELS,
        )
        return full, add(gram, over_rank(gram))

    buffers = [pltpu.VMEM(a.shape, BF) for a in (probes, *uppers)]
    (own,) = call(
        first_kernel,
        [S((LEVELS * c, k), BF)],
        (place, probes, *uppers),
        2 * n * LEVELS * k * c,
        [*buffers, sems((LEVELS + 1, CHUNKS))],
        LEVELS + 1,
    )
    (packed,) = call(join_kernel, [p_shape], (place, own, over_rank(own)), 0)
    packed, lowers, probes, leaves = lax.optimization_barrier((packed, lowers, probes, leaves))
    summed = packed
    lower, lower_gram = prepared(lowers)
    upper, upper_gram = prepared(uppers)
    field_flops = 4 * half * wide * c
    y, s = call(start_kernel, [y_shape, s_shape], (place, probes, leaves, lower), field_flops // 2)
    applies = 2 * PASSES
    source = 0
    for step in range(applies):
        flipped = step % 2 == 0
        found, source = siblings_of(place, packed, summed, source)
        holders = [f[2] for f in found]
        pieces = [x for f in found for x in f[:2]]
        if step + 1 == applies:
            rest = pltpu.VMEM((c, wide - 2 * k), BF)
            (y,) = call(
                lambda *r: most_kernel(holders[1:], *r), [y_shape], (place, *pieces[2:], upper, y), field_flops // 3, [rest]
            )
            (out,) = call(
                lambda *r: last_kernel(holders[:1], *r),
                [S((half, c), BF)],
                (place, *pieces[:2], upper, y),
                field_flops // 6,
                [pltpu.VMEM((c, 2 * k), BF)],
            )
            return out
        there = over_rank(s)
        early = [f[0] if f[2] == source else f[1] for f in found]
        gram = lower_gram if flipped else upper_gram
        (packed,) = call(next_kernel, [p_shape], (place, *early, gram, s, there), 2 * wide * wide * c)
        factor, after = (lower, upper) if flipped else (upper, lower)
        summed, q = call(
            lambda *r: again_kernel(holders, *r), [p_shape, s_shape], (place, *pieces, gram, s, there), 2 * wide * wide * c
        )
        if step + 2 == applies:
            (y,) = call(
                lambda *r: late_kernel(not flipped, *r), [y_shape], (place, q, factor, y, leaves), field_flops // 2
            )
        else:
            y, s = call(
                lambda *r: field_kernel(not flipped, *r),
                [y_shape, s_shape],
                (place, q, factor, y, leaves, after),
                field_flops,
            )


def solution(mesh):
    rows = P(("parts", "rows", "cols"), None)
    split = P(("parts", "rows", "cols"), "rank")
    every = ("parts", "rows", "cols", "rank")
    in_specs = (rows,) + (split,) * 6 + (P(every, None, None),)

    return jax.shard_map(local, mesh=mesh, in_specs=in_specs, out_specs=P(every, None), check_vma=False)
```

```python
import jax
import jax.numpy as jnp
from jax import lax
from jax.experimental import pallas as pl
from jax.experimental.pallas import tpu as pltpu
from jax.sharding import PartitionSpec as P


PASSES = 2
LEVELS = 3
CHUNKS = 4
BLOCKS = tuple((i, j) for i in range(LEVELS) for j in range(i + 1))
BF = jnp.bfloat16
F32 = jnp.float32
VMEM_BYTES = 12 * 2**20


def mm(a, b, ca, cb):
    return lax.dot_general(a, b, (((ca,), (cb,)), ((), ())), preferred_element_type=F32)


def call(kernel, outs, args, flops, scratch=(), far=0):
    vm = pl.BlockSpec(memory_space=pltpu.VMEM)
    hbm = pl.BlockSpec(memory_space=pltpu.HBM)
    near, distant = args[: len(args) - far], args[len(args) - far :]
    moved = sum(a.size * a.dtype.itemsize for a in args[1:]) + sum(o.size * o.dtype.itemsize for o in outs)
    return pl.pallas_call(
        kernel,
        out_shape=outs,
        in_specs=[pl.BlockSpec(memory_space=pltpu.SMEM)] + [vm] * (len(args) - 1 - far) + [hbm] * far,
        out_specs=[vm] * len(outs),
        scratch_shapes=list(scratch),
        cost_estimate=pl.CostEstimate(flops=flops, bytes_accessed=moved, transcendentals=0),
        compiler_params=pltpu.CompilerParams(vmem_limit_bytes=VMEM_BYTES),
    )(*near, *(pltpu.with_memory_space_constraint(a, pltpu.HBM) for a in distant))


def at(start, size):
    return pl.ds(pl.multiple_of(start, size), size)


def first_kernel(place, *refs):
    sources, out, buffers, sems = refs[: LEVELS + 1], refs[LEVELS + 1], refs[LEVELS + 2 : -1], refs[-1]
    rows = sources[0].shape[0] // CHUNKS
    copies = [
        [
            pltpu.make_async_copy(a.at[pl.ds(j * rows, rows), :], b.at[pl.ds(j * rows, rows), :], sems.at[i, j])
            for j in range(CHUNKS)
        ]
        for i, (a, b) in enumerate(zip(sources, buffers))
    ]
    for group in copies:
        for copy in group:
            copy.start()
    for copy in copies[0]:
        copy.wait()
    zt = buffers[0][...].T
    c = zt.shape[0]
    for level in range(LEVELS):
        for copy in copies[1 + level]:
            copy.wait()
        out[level * c : (level + 1) * c, :] = mm(zt, buffers[1 + level][...], 1, 0).astype(BF)


def pack_kernel(place, *refs):
    sources, out = refs[:LEVELS], refs[LEVELS]
    half = out.shape[0] // LEVELS
    for i, a in enumerate(sources):
        out[i * half : (i + 1) * half, :] = a[at((1 - place[0]) * half, half), :]


def beside_kernel(place, left, right, out):
    k = left.shape[1]
    out[:, :k] = left[...]
    out[:, k:] = right[...]


def join_kernel(place, own, other, out):
    k = own.shape[1]
    me = place[0]
    out[:, at(me * k, k)] = own[...]
    out[:, at((1 - me) * k, k)] = other[...]


def gram_kernel(place, other, *refs):
    own, (full, gram) = refs[:LEVELS], refs[LEVELS:]
    half, k = other.shape[0] // LEVELS, other.shape[1]
    me = place[0]
    for level in range(LEVELS):
        full[:, at((2 * level + me) * k, k)] = own[level][at(me * half, half), :]
        full[:, at((2 * level + 1 - me) * k, k)] = other[level * half : (level + 1) * half, :]
    wide = 2 * k
    for n, (i, j) in enumerate(BLOCKS):
        if j == 0:
            left = full[:, i * wide : (i + 1) * wide].T
        gram[n * wide : (n + 1) * wide, :] = mm(left, full[:, j * wide : (j + 1) * wide], 1, 0).astype(BF)


def whole_kernel(place, mine, other, out):
    k = mine.shape[1]
    for n, (i, j) in enumerate(BLOCKS):
        block = add(mine[n * k : (n + 1) * k, :], other[n * k : (n + 1) * k, :])
        out[i * k : (i + 1) * k, j * k : (j + 1) * k] = block
        if j < i:
            out[j * k : (j + 1) * k, i * k : (i + 1) * k] = block.T


def join_siblings(one, more, two, three, joined):
    k = one.shape[1]
    joined[:, :k] = add(one[...], more[...])
    joined[:, k : 2 * k] = two[...]
    joined[:, 2 * k :] = three[...]


def next_kernel(place, one, more, two, three, gram, here, there, out, joined):
    join_siblings(one, more, two, three, joined)
    c, k = one.shape
    for level in range(LEVELS):
        cols = slice(level * k, (level + 1) * k)
        total = here[:, cols].astype(F32) + there[:, cols].astype(F32) + mm(joined[...], gram[:, cols], 1, 0)
        out[level * c : (level + 1) * c, :] = total.astype(BF)


def again_kernel(holder, place, early, mine, other, gram, here, there, out, joined):
    @pl.when(place[0] == holder)
    def _():
        out[...] = early[...]
        joined[...] = mine[...]

    @pl.when(place[0] != holder)
    def _():
        joined[...] = other[...]
        c, k = out.shape[0] // LEVELS, out.shape[1]
        for level in range(LEVELS):
            cols = slice(level * k, (level + 1) * k)
            total = here[:, cols].astype(F32) + there[:, cols].astype(F32) + mm(joined[...], gram[:, cols], 1, 0)
            out[level * c : (level + 1) * c, :] = total.astype(BF)


def sum_kernel(source, place, summed, received, relayed, out):
    n = out.shape[0]

    @pl.when(place[0] == source)
    def _():
        out[...] = add(summed[:n, :], relayed[:n, :])

    @pl.when(place[0] != source)
    def _():
        out[...] = add(summed[:n, :], received[:n, :])


def leaf_terms(z, leaves, flipped, out):
    size = leaves.shape[1]
    for q in range(leaves.shape[0]):
        rows = slice(q * size, (q + 1) * size)
        out[rows, :] = mm(leaves[q], z[rows, :], 0 if flipped else 1, 0)


def start_kernel(place, z, leaves, after, y, s):
    half = y.shape[0]
    leaf_terms(z[at(place[0] * half, half), :], leaves, True, y)
    s[...] = mm(y[...].astype(BF).T, after[...], 1, 0).astype(BF)


def project_kernel(place, y, after, s):
    s[...] = mm(y[...].astype(BF).T, after[...], 1, 0).astype(BF)


def field_kernel(flipped, place, q, factor, was, leaves, y):
    z = (mm(factor[...], q[...], 1, 1) + was[...]).astype(BF)
    leaf_terms(z, leaves, flipped, y)


def siblings_kernel(place, one, more, two, three, joined):
    join_siblings(one, more, two, three, joined)


def last_kernel(holder, place, mine, other, factor, was, out, joined):
    @pl.when(place[0] == holder)
    def _():
        joined[...] = mine[...]

    @pl.when(place[0] != holder)
    def _():
        joined[...] = other[...]

    out[...] = (mm(factor[...], joined[...], 1, 1) + was[...]).astype(BF)


def one_way(value, mask, source):
    chips = lax.axis_size(("rows", "cols"))
    away = [(2 * p + source, 2 * (p ^ mask) + 1 - source) for p in range(chips)]
    home = [(2 * p + 1 - source, 2 * p + source) for p in range(chips)]
    return lax.ppermute(value, ("rows", "cols", "rank"), away + home)


def over_rank(value):
    return lax.ppermute(value, "rank", [(0, 1), (1, 0)])


def add(a, b):
    return (a.astype(F32) + b.astype(F32)).astype(BF)


def gathered(place, packed, summed, source):
    chips = lax.axis_size(("rows", "cols"))
    stride = 1
    while stride < chips // 2**LEVELS:
        received = one_way(packed, stride, source)
        relayed = over_rank(received)
        packed = add(summed, received)
        shape = jax.ShapeDtypeStruct(packed.shape, BF)
        (summed,) = call(
            lambda *r, source=source: sum_kernel(source, *r), [shape], (place, summed, received, relayed), 0
        )
        source, stride = 1 - source, 2 * stride
    return packed, summed, source, stride


def siblings_of(packed, summed, source, stride, received=None):
    c = packed.shape[0] // LEVELS
    if received is None:
        received = one_way(packed[: 2 * c], stride, source)
    three = one_way(summed[2 * c :], stride, 1 - source)
    both = add(summed[: 2 * c], received)
    one = one_way(both[:c], 6 * stride, 1 - source)
    more = one_way(both[:c], 4 * stride, 1 - source)
    two = one_way(both[c:], 2 * stride, 1 - source)
    return one, more, two, three


def local(probes, basis_one, basis_two, basis_three, coeff_one, coeff_two, coeff_three, leaves):
    place = lax.axis_index("rank").reshape(1)
    n, c = probes.shape
    half = n // 2
    k = basis_one.shape[1]
    wide = 2 * k * LEVELS
    S = jax.ShapeDtypeStruct
    p_shape, y_shape, s_shape = S((LEVELS * c, 2 * k), BF), S((half, c), F32), S((c, wide), BF)
    sems = pltpu.SemaphoreType.DMA
    uppers = (basis_one, basis_two, basis_three)
    lowers = (coeff_one, coeff_two, coeff_three)

    def prepared(factors):
        (sent,) = call(pack_kernel, [S((LEVELS * half, k), BF)], (place, *factors), 0)
        other = over_rank(sent)
        full, gram = call(
            gram_kernel,
            [S((half, wide), BF), S((len(BLOCKS) * 2 * k, 2 * k), BF)],
            (place, other, *factors),
            half * wide * wide * 3 // 2,
        )
        other = over_rank(gram)
        (gram,) = call(whole_kernel, [S((wide, wide), BF)], (place, gram, other), 0)
        return full, gram

    buffers = [pltpu.VMEM(a.shape, BF) for a in (probes, *uppers)]
    (own,) = call(
        first_kernel,
        [S((LEVELS * c, k), BF)],
        (place, probes, *uppers),
        2 * n * LEVELS * k * c,
        [*buffers, sems((LEVELS + 1, CHUNKS))],
        LEVELS + 1,
    )
    other = over_rank(own)
    (summed,) = call(join_kernel, [p_shape], (place, own, other), 0)
    packed, received = summed, None
    if lax.axis_size(("rows", "cols")) == 2**LEVELS:
        left = one_way(own[: 2 * c], 1, 0)
        right = one_way(other[: 2 * c], 1, 0)
        (received,) = call(beside_kernel, [S((2 * c, 2 * k), BF)], (place, left, right), 0)
    lower, lower_gram = prepared(lowers)
    upper, upper_gram = prepared(uppers)
    field_flops = 4 * half * wide * c
    y, s = call(start_kernel, [y_shape, s_shape], (place, probes, leaves, lower), field_flops // 2)
    applies = 2 * PASSES
    source = 0
    for step in range(applies):
        flipped = step % 2 == 0
        packed, summed, source, stride = gathered(place, packed, summed, source)
        pieces = siblings_of(packed, summed, source, stride, received)
        received = None
        if step + 1 == applies:
            (q,) = call(siblings_kernel, [s_shape], (place, *pieces), 0)
            other = over_rank(q)
            (out,) = call(
                lambda *r: last_kernel(source, *r),
                [S((half, c), BF)],
                (place, q, other, upper, y),
                field_flops // 2,
                [pltpu.VMEM((c, wide), BF)],
            )
            return out
        there = over_rank(s)
        gram = lower_gram if flipped else upper_gram
        factor, after = (lower, upper) if flipped else (upper, lower)
        packed, q = call(next_kernel, [p_shape, s_shape], (place, *pieces, gram, s, there), 2 * wide * wide * c)
        other = over_rank(q)
        summed, q = call(
            lambda *r: again_kernel(source, *r),
            [p_shape, s_shape],
            (place, packed, q, other, gram, s, there),
            2 * wide * wide * c,
        )
        (y,) = call(lambda *r: field_kernel(not flipped, *r), [y_shape], (place, q, factor, y, leaves), field_flops // 2)
        if step + 2 < applies:
            (s,) = call(project_kernel, [s_shape], (place, y, after), field_flops // 2)


def solution(mesh):
    rows = P(("parts", "rows", "cols"), None)
    split = P(("parts", "rows", "cols"), "rank")
    every = ("parts", "rows", "cols", "rank")
    in_specs = (rows,) + (split,) * 6 + (P(every, None, None),)

    return jax.shard_map(local, mesh=mesh, in_specs=in_specs, out_specs=P(every, None), check_vma=False)
```

```python
import jax
import jax.numpy as jnp
from jax import lax
from jax.experimental import pallas as pl
from jax.experimental.pallas import tpu as pltpu
from jax.sharding import PartitionSpec as P


PASSES = 2
LEVELS = 3
CHUNKS = 4
BLOCKS = tuple((i, j) for i in range(LEVELS) for j in range(i + 1))
BF = jnp.bfloat16
F32 = jnp.float32
VMEM_BYTES = 12 * 2**20


def mm(a, b, ca, cb):
    return lax.dot_general(a, b, (((ca,), (cb,)), ((), ())), preferred_element_type=F32)


def call(kernel, outs, args, flops, scratch=(), far=0):
    vm = pl.BlockSpec(memory_space=pltpu.VMEM)
    hbm = pl.BlockSpec(memory_space=pltpu.HBM)
    near, distant = args[: len(args) - far], args[len(args) - far :]
    moved = sum(a.size * a.dtype.itemsize for a in args[1:]) + sum(o.size * o.dtype.itemsize for o in outs)
    return pl.pallas_call(
        kernel,
        out_shape=outs,
        in_specs=[pl.BlockSpec(memory_space=pltpu.SMEM)] + [vm] * (len(args) - 1 - far) + [hbm] * far,
        out_specs=[vm] * len(outs),
        scratch_shapes=list(scratch),
        cost_estimate=pl.CostEstimate(flops=flops, bytes_accessed=moved, transcendentals=0),
        compiler_params=pltpu.CompilerParams(vmem_limit_bytes=VMEM_BYTES),
    )(*near, *(pltpu.with_memory_space_constraint(a, pltpu.HBM) for a in distant))


def at(start, size):
    return pl.ds(pl.multiple_of(start, size), size)


def first_kernel(place, *refs):
    sources, out, buffers, sems = refs[: LEVELS + 1], refs[LEVELS + 1], refs[LEVELS + 2 : -1], refs[-1]
    rows = sources[0].shape[0] // CHUNKS
    copies = [
        [
            pltpu.make_async_copy(a.at[pl.ds(j * rows, rows), :], b.at[pl.ds(j * rows, rows), :], sems.at[i, j])
            for j in range(CHUNKS)
        ]
        for i, (a, b) in enumerate(zip(sources, buffers))
    ]
    for group in copies:
        for copy in group:
            copy.start()
    for copy in copies[0]:
        copy.wait()
    zt = buffers[0][...].T
    c = zt.shape[0]
    for level in range(LEVELS):
        for copy in copies[1 + level]:
            copy.wait()
        out[level * c : (level + 1) * c, :] = mm(zt, buffers[1 + level][...], 1, 0).astype(BF)


def pack_kernel(place, *refs):
    sources, out = refs[:LEVELS], refs[LEVELS]
    half = out.shape[0] // LEVELS
    for i, a in enumerate(sources):
        out[i * half : (i + 1) * half, :] = a[at((1 - place[0]) * half, half), :]


def beside_kernel(place, left, right, out):
    k = left.shape[1]
    out[:, :k] = left[...]
    out[:, k:] = right[...]


def join_kernel(place, own, other, out):
    k = own.shape[1]
    me = place[0]
    out[:, at(me * k, k)] = own[...]
    out[:, at((1 - me) * k, k)] = other[...]


def gram_kernel(place, other, *refs):
    own, (full, gram) = refs[:LEVELS], refs[LEVELS:]
    half, k = other.shape[0] // LEVELS, other.shape[1]
    me = place[0]
    for level in range(LEVELS):
        full[:, at((2 * level + me) * k, k)] = own[level][at(me * half, half), :]
        full[:, at((2 * level + 1 - me) * k, k)] = other[level * half : (level + 1) * half, :]
    wide = 2 * k
    for n, (i, j) in enumerate(BLOCKS):
        if j == 0:
            left = full[:, i * wide : (i + 1) * wide].T
        gram[n * wide : (n + 1) * wide, :] = mm(left, full[:, j * wide : (j + 1) * wide], 1, 0).astype(BF)


def whole_kernel(place, mine, other, out):
    k = mine.shape[1]
    for n, (i, j) in enumerate(BLOCKS):
        block = add(mine[n * k : (n + 1) * k, :], other[n * k : (n + 1) * k, :])
        out[i * k : (i + 1) * k, j * k : (j + 1) * k] = block
        if j < i:
            out[j * k : (j + 1) * k, i * k : (i + 1) * k] = block.T


def join_siblings(one, more, two, three, joined):
    k = one.shape[1]
    joined[:, :k] = add(one[...], more[...])
    joined[:, k : 2 * k] = two[...]
    joined[:, 2 * k :] = three[...]


def next_kernel(place, one, more, two, three, gram, here, there, out, joined):
    join_siblings(one, more, two, three, joined)
    c, k = one.shape
    for level in range(LEVELS):
        cols = slice(level * k, (level + 1) * k)
        total = here[:, cols].astype(F32) + there[:, cols].astype(F32) + mm(joined[...], gram[:, cols], 1, 0)
        out[level * c : (level + 1) * c, :] = total.astype(BF)


def again_kernel(holder, place, early, other, gram, here, there, out):
    @pl.when(place[0] == holder)
    def _():
        out[...] = early[...]

    @pl.when(place[0] != holder)
    def _():
        c, k = out.shape[0] // LEVELS, out.shape[1]
        for level in range(LEVELS):
            cols = slice(level * k, (level + 1) * k)
            total = here[:, cols].astype(F32) + there[:, cols].astype(F32) + mm(other[...], gram[:, cols], 1, 0)
            out[level * c : (level + 1) * c, :] = total.astype(BF)


def pick_kernel(holder, place, mine, other, out):
    @pl.when(place[0] == holder)
    def _():
        out[...] = mine[...]

    @pl.when(place[0] != holder)
    def _():
        out[...] = other[...]


def sum_kernel(source, place, summed, received, relayed, out):
    n = out.shape[0]

    @pl.when(place[0] == source)
    def _():
        out[...] = add(summed[:n, :], relayed[:n, :])

    @pl.when(place[0] != source)
    def _():
        out[...] = add(summed[:n, :], received[:n, :])


def leaf_terms(z, leaves, flipped, out):
    size = leaves.shape[1]
    for q in range(leaves.shape[0]):
        rows = slice(q * size, (q + 1) * size)
        out[rows, :] = mm(leaves[q], z[rows, :], 0 if flipped else 1, 0)


def start_kernel(place, z, leaves, after, y, s):
    half = y.shape[0]
    leaf_terms(z[at(place[0] * half, half), :], leaves, True, y)
    s[...] = mm(y[...].astype(BF).T, after[...], 1, 0).astype(BF)


def project_kernel(place, y, after, s):
    s[...] = mm(y[...].astype(BF).T, after[...], 1, 0).astype(BF)


def field_kernel(flipped, place, q, factor, was, leaves, y):
    z = (mm(factor[...], q[...], 1, 1) + was[...]).astype(BF)
    leaf_terms(z, leaves, flipped, y)


def siblings_kernel(place, one, more, two, three, joined):
    join_siblings(one, more, two, three, joined)


def last_kernel(holder, place, mine, other, factor, was, out, joined):
    @pl.when(place[0] == holder)
    def _():
        joined[...] = mine[...]

    @pl.when(place[0] != holder)
    def _():
        joined[...] = other[...]

    out[...] = (mm(factor[...], joined[...], 1, 1) + was[...]).astype(BF)


def one_way(value, mask, source):
    chips = lax.axis_size(("rows", "cols"))
    away = [(2 * p + source, 2 * (p ^ mask) + 1 - source) for p in range(chips)]
    home = [(2 * p + 1 - source, 2 * p + source) for p in range(chips)]
    return lax.ppermute(value, ("rows", "cols", "rank"), away + home)


def over_rank(value):
    return lax.ppermute(value, "rank", [(0, 1), (1, 0)])


def add(a, b):
    return (a.astype(F32) + b.astype(F32)).astype(BF)


def gathered(place, packed, summed, source):
    chips = lax.axis_size(("rows", "cols"))
    stride = 1
    while stride < chips // 2**LEVELS:
        received = one_way(packed, stride, source)
        relayed = over_rank(received)
        packed = add(summed, received)
        shape = jax.ShapeDtypeStruct(packed.shape, BF)
        (summed,) = call(
            lambda *r, source=source: sum_kernel(source, *r), [shape], (place, summed, received, relayed), 0
        )
        source, stride = 1 - source, 2 * stride
    return packed, summed, source, stride


def siblings_of(packed, summed, source, stride, received=None):
    c = packed.shape[0] // LEVELS
    if received is None:
        received = one_way(packed[: 2 * c], stride, source)
    three = one_way(summed[2 * c :], stride, 1 - source)
    both = add(summed[: 2 * c], received)
    one = one_way(both[:c], 6 * stride, 1 - source)
    more = one_way(both[:c], 4 * stride, 1 - source)
    two = one_way(both[c:], 2 * stride, 1 - source)
    return one, more, two, three


def local(probes, basis_one, basis_two, basis_three, coeff_one, coeff_two, coeff_three, leaves):
    place = lax.axis_index("rank").reshape(1)
    n, c = probes.shape
    half = n // 2
    k = basis_one.shape[1]
    wide = 2 * k * LEVELS
    S = jax.ShapeDtypeStruct
    p_shape, y_shape, s_shape = S((LEVELS * c, 2 * k), BF), S((half, c), F32), S((c, wide), BF)
    sems = pltpu.SemaphoreType.DMA
    uppers = (basis_one, basis_two, basis_three)
    lowers = (coeff_one, coeff_two, coeff_three)

    def prepared(factors):
        (sent,) = call(pack_kernel, [S((LEVELS * half, k), BF)], (place, *factors), 0)
        other = over_rank(sent)
        full, gram = call(
            gram_kernel,
            [S((half, wide), BF), S((len(BLOCKS) * 2 * k, 2 * k), BF)],
            (place, other, *factors),
            half * wide * wide * 3 // 2,
        )
        other = over_rank(gram)
        (gram,) = call(whole_kernel, [S((wide, wide), BF)], (place, gram, other), 0)
        return full, gram

    buffers = [pltpu.VMEM(a.shape, BF) for a in (probes, *uppers)]
    (own,) = call(
        first_kernel,
        [S((LEVELS * c, k), BF)],
        (place, probes, *uppers),
        2 * n * LEVELS * k * c,
        [*buffers, sems((LEVELS + 1, CHUNKS))],
        LEVELS + 1,
    )
    other = over_rank(own)
    (summed,) = call(join_kernel, [p_shape], (place, own, other), 0)
    packed, received = summed, None
    if lax.axis_size(("rows", "cols")) == 2**LEVELS:
        left = one_way(own[: 2 * c], 1, 0)
        right = one_way(other[: 2 * c], 1, 0)
        (received,) = call(beside_kernel, [S((2 * c, 2 * k), BF)], (place, left, right), 0)
    lower, lower_gram = prepared(lowers)
    upper, upper_gram = prepared(uppers)
    field_flops = 4 * half * wide * c
    y, s = call(start_kernel, [y_shape, s_shape], (place, probes, leaves, lower), field_flops // 2)
    applies = 2 * PASSES
    source = 0
    for step in range(applies):
        flipped = step % 2 == 0
        packed, summed, source, stride = gathered(place, packed, summed, source)
        pieces = siblings_of(packed, summed, source, stride, received)
        received = None
        if step + 1 == applies:
            (q,) = call(siblings_kernel, [s_shape], (place, *pieces), 0)
            other = over_rank(q)
            (out,) = call(
                lambda *r: last_kernel(source, *r),
                [S((half, c), BF)],
                (place, q, other, upper, y),
                field_flops // 2,
                [pltpu.VMEM((c, wide), BF)],
            )
            return out
        there = over_rank(s)
        gram = lower_gram if flipped else upper_gram
        factor, after = (lower, upper) if flipped else (upper, lower)
        packed, q = call(next_kernel, [p_shape, s_shape], (place, *pieces, gram, s, there), 2 * wide * wide * c)
        other = over_rank(q)
        (summed,) = call(
            lambda *r: again_kernel(source, *r), [p_shape], (place, packed, other, gram, s, there), 2 * wide * wide * c
        )
        (q,) = call(lambda *r: pick_kernel(source, *r), [s_shape], (place, q, other), 0)
        (y,) = call(lambda *r: field_kernel(not flipped, *r), [y_shape], (place, q, factor, y, leaves), field_flops // 2)
        if step + 2 < applies:
            (s,) = call(project_kernel, [s_shape], (place, y, after), field_flops // 2)


def solution(mesh):
    rows = P(("parts", "rows", "cols"), None)
    split = P(("parts", "rows", "cols"), "rank")
    every = ("parts", "rows", "cols", "rank")
    in_specs = (rows,) + (split,) * 6 + (P(every, None, None),)

    return jax.shard_map(local, mesh=mesh, in_specs=in_specs, out_specs=P(every, None), check_vma=False)
```

```python
import jax
import jax.numpy as jnp
from jax import lax
from jax.experimental import pallas as pl
from jax.experimental.pallas import tpu as pltpu
from jax.sharding import PartitionSpec as P


PASSES = 2
LEVELS = 3
BLOCKS = tuple((i, j) for i in range(LEVELS) for j in range(i + 1))
BF = jnp.bfloat16
F32 = jnp.float32
VMEM_BYTES = 12 * 2**20


def mm(a, b, ca, cb):
    return lax.dot_general(a, b, (((ca,), (cb,)), ((), ())), preferred_element_type=F32)


def call(kernel, outs, args, flops, scratch=(), far=0):
    vm = pl.BlockSpec(memory_space=pltpu.VMEM)
    hbm = pl.BlockSpec(memory_space=pltpu.HBM)
    near, distant = args[: len(args) - far], args[len(args) - far :]
    moved = sum(a.size * a.dtype.itemsize for a in args[1:]) + sum(o.size * o.dtype.itemsize for o in outs)
    return pl.pallas_call(
        kernel,
        out_shape=outs,
        in_specs=[pl.BlockSpec(memory_space=pltpu.SMEM)] + [vm] * (len(args) - 1 - far) + [hbm] * far,
        out_specs=[vm] * len(outs),
        scratch_shapes=list(scratch),
        cost_estimate=pl.CostEstimate(flops=flops, bytes_accessed=moved, transcendentals=0),
        compiler_params=pltpu.CompilerParams(vmem_limit_bytes=VMEM_BYTES),
    )(*near, *(pltpu.with_memory_space_constraint(a, pltpu.HBM) for a in distant))


def at(start, size):
    return pl.ds(pl.multiple_of(start, size), size)


def first_kernel(place, *refs):
    sources, out, buffers, sems = refs[: LEVELS + 1], refs[LEVELS + 1], refs[LEVELS + 2 : -1], refs[-1]
    copies = [pltpu.make_async_copy(a, b, sems.at[i]) for i, (a, b) in enumerate(zip(sources, buffers))]
    for copy in copies:
        copy.start()
    copies[0].wait()
    zt = buffers[0][...].T
    c = zt.shape[0]
    for level in range(LEVELS):
        copies[1 + level].wait()
        out[level * c : (level + 1) * c, :] = mm(zt, buffers[1 + level][...], 1, 0).astype(BF)


def pack_kernel(place, *refs):
    sources, out = refs[:LEVELS], refs[LEVELS]
    half = out.shape[0] // LEVELS
    for i, a in enumerate(sources):
        out[i * half : (i + 1) * half, :] = a[at((1 - place[0]) * half, half), :]


def beside_kernel(place, left, right, out):
    k = left.shape[1]
    out[:, :k] = left[...]
    out[:, k:] = right[...]


def join_kernel(place, own, other, out):
    k = own.shape[1]
    me = place[0]
    out[:, at(me * k, k)] = own[...]
    out[:, at((1 - me) * k, k)] = other[...]


def gram_kernel(place, other, *refs):
    own, (full, gram) = refs[:LEVELS], refs[LEVELS:]
    half, k = other.shape[0] // LEVELS, other.shape[1]
    me = place[0]
    for level in range(LEVELS):
        full[:, at((2 * level + me) * k, k)] = own[level][at(me * half, half), :]
        full[:, at((2 * level + 1 - me) * k, k)] = other[level * half : (level + 1) * half, :]
    wide = 2 * k
    for n, (i, j) in enumerate(BLOCKS):
        if j == 0:
            left = full[:, i * wide : (i + 1) * wide].T
        gram[n * wide : (n + 1) * wide, :] = mm(left, full[:, j * wide : (j + 1) * wide], 1, 0).astype(BF)


def whole_kernel(place, mine, other, out):
    k = mine.shape[1]
    for n, (i, j) in enumerate(BLOCKS):
        block = add(mine[n * k : (n + 1) * k, :], other[n * k : (n + 1) * k, :])
        out[i * k : (i + 1) * k, j * k : (j + 1) * k] = block
        if j < i:
            out[j * k : (j + 1) * k, i * k : (i + 1) * k] = block.T


def join_siblings(one, more, two, three, joined):
    k = one.shape[1]
    joined[:, :k] = add(one[...], more[...])
    joined[:, k : 2 * k] = two[...]
    joined[:, 2 * k :] = three[...]


def next_kernel(place, one, more, two, three, gram, here, there, out, joined):
    join_siblings(one, more, two, three, joined)
    c, k = one.shape
    for level in range(LEVELS):
        cols = slice(level * k, (level + 1) * k)
        total = here[:, cols].astype(F32) + there[:, cols].astype(F32) + mm(joined[...], gram[:, cols], 1, 0)
        out[level * c : (level + 1) * c, :] = total.astype(BF)


def again_kernel(holder, place, early, other, gram, here, there, out):
    @pl.when(place[0] == holder)
    def _():
        out[...] = early[...]

    @pl.when(place[0] != holder)
    def _():
        c, k = out.shape[0] // LEVELS, out.shape[1]
        for level in range(LEVELS):
            cols = slice(level * k, (level + 1) * k)
            total = here[:, cols].astype(F32) + there[:, cols].astype(F32) + mm(other[...], gram[:, cols], 1, 0)
            out[level * c : (level + 1) * c, :] = total.astype(BF)


def pick_kernel(holder, place, mine, other, out):
    @pl.when(place[0] == holder)
    def _():
        out[...] = mine[...]

    @pl.when(place[0] != holder)
    def _():
        out[...] = other[...]


def sum_kernel(source, place, summed, received, relayed, out):
    n = out.shape[0]

    @pl.when(place[0] == source)
    def _():
        out[...] = add(summed[:n, :], relayed[:n, :])

    @pl.when(place[0] != source)
    def _():
        out[...] = add(summed[:n, :], received[:n, :])


def leaf_terms(z, leaves, flipped, out):
    size = leaves.shape[1]
    for q in range(leaves.shape[0]):
        rows = slice(q * size, (q + 1) * size)
        out[rows, :] = mm(leaves[q], z[rows, :], 0 if flipped else 1, 0)


def start_kernel(place, z, leaves, after, y, s):
    half = y.shape[0]
    leaf_terms(z[at(place[0] * half, half), :], leaves, True, y)
    s[...] = mm(y[...].astype(BF).T, after[...], 1, 0).astype(BF)


def project_kernel(place, y, after, s):
    s[...] = mm(y[...].astype(BF).T, after[...], 1, 0).astype(BF)


def field_kernel(flipped, place, q, factor, was, leaves, y):
    z = (mm(factor[...], q[...], 1, 1) + was[...]).astype(BF)
    leaf_terms(z, leaves, flipped, y)


def siblings_kernel(place, one, more, two, out):
    k = one.shape[1]
    out[:, :k] = add(one[...], more[...])
    out[:, k:] = two[...]


def most_kernel(holder, place, three, other, factor, was, y, joined):
    pick_kernel(holder, place, three, other, joined)
    y[...] = mm(factor[:, -joined.shape[1] :], joined[...], 1, 1) + was[...]


def last_kernel(holder, place, mine, other, factor, was, out, joined):
    pick_kernel(holder, place, mine, other, joined)
    out[...] = (mm(factor[:, : joined.shape[1]], joined[...], 1, 1) + was[...]).astype(BF)


def one_way(value, mask, source):
    chips = lax.axis_size(("rows", "cols"))
    away = [(2 * p + source, 2 * (p ^ mask) + 1 - source) for p in range(chips)]
    home = [(2 * p + 1 - source, 2 * p + source) for p in range(chips)]
    return lax.ppermute(value, ("rows", "cols", "rank"), away + home)


def over_rank(value):
    return lax.ppermute(value, "rank", [(0, 1), (1, 0)])


def add(a, b):
    return (a.astype(F32) + b.astype(F32)).astype(BF)


def gathered(place, packed, summed, source):
    chips = lax.axis_size(("rows", "cols"))
    stride = 1
    while stride < chips // 2**LEVELS:
        received = one_way(packed, stride, source)
        relayed = over_rank(received)
        packed = add(summed, received)
        shape = jax.ShapeDtypeStruct(packed.shape, BF)
        (summed,) = call(
            lambda *r, source=source: sum_kernel(source, *r), [shape], (place, summed, received, relayed), 0
        )
        source, stride = 1 - source, 2 * stride
    return packed, summed, source, stride


def siblings_of(packed, summed, source, stride, received=None):
    c = packed.shape[0] // LEVELS
    if received is None:
        received = one_way(packed[: 2 * c], stride, source)
    three = one_way(summed[2 * c :], stride, 1 - source)
    both = add(summed[: 2 * c], received)
    one = one_way(both[:c], 6 * stride, 1 - source)
    more = one_way(both[:c], 4 * stride, 1 - source)
    two = one_way(both[c:], 2 * stride, 1 - source)
    return one, more, two, three


def local(probes, basis_one, basis_two, basis_three, coeff_one, coeff_two, coeff_three, leaves):
    place = lax.axis_index("rank").reshape(1)
    n, c = probes.shape
    half = n // 2
    k = basis_one.shape[1]
    wide = 2 * k * LEVELS
    S = jax.ShapeDtypeStruct
    p_shape, y_shape, s_shape = S((LEVELS * c, 2 * k), BF), S((half, c), F32), S((c, wide), BF)
    sems = pltpu.SemaphoreType.DMA
    uppers = (basis_one, basis_two, basis_three)
    lowers = (coeff_one, coeff_two, coeff_three)

    def prepared(factors):
        (sent,) = call(pack_kernel, [S((LEVELS * half, k), BF)], (place, *factors), 0)
        other = over_rank(sent)
        full, gram = call(
            gram_kernel,
            [S((half, wide), BF), S((len(BLOCKS) * 2 * k, 2 * k), BF)],
            (place, other, *factors),
            half * wide * wide * 3 // 2,
        )
        other = over_rank(gram)
        (gram,) = call(whole_kernel, [S((wide, wide), BF)], (place, gram, other), 0)
        return full, gram

    buffers = [pltpu.VMEM(a.shape, BF) for a in (probes, *uppers)]
    (own,) = call(
        first_kernel,
        [S((LEVELS * c, k), BF)],
        (place, probes, *uppers),
        2 * n * LEVELS * k * c,
        [*buffers, sems((LEVELS + 1,))],
        LEVELS + 1,
    )
    other = over_rank(own)
    (summed,) = call(join_kernel, [p_shape], (place, own, other), 0)
    packed, received = summed, None
    if lax.axis_size(("rows", "cols")) == 2**LEVELS:
        left = one_way(own[: 2 * c], 1, 0)
        right = one_way(other[: 2 * c], 1, 0)
        (received,) = call(beside_kernel, [S((2 * c, 2 * k), BF)], (place, left, right), 0)
    lower, lower_gram = prepared(lowers)
    upper, upper_gram = prepared(uppers)
    field_flops = 4 * half * wide * c
    y, s = call(start_kernel, [y_shape, s_shape], (place, probes, leaves, lower), field_flops // 2)
    applies = 2 * PASSES
    source = 0
    for step in range(applies):
        flipped = step % 2 == 0
        packed, summed, source, stride = gathered(place, packed, summed, source)
        pieces = siblings_of(packed, summed, source, stride, received)
        received = None
        if step + 1 == applies:
            one, more, two, three = pieces
            other = over_rank(three)
            (y,) = call(
                lambda *r: most_kernel(source, *r),
                [y_shape],
                (place, three, other, upper, y),
                field_flops // 6,
                [pltpu.VMEM((c, 2 * k), BF)],
            )
            (q,) = call(siblings_kernel, [S((c, 4 * k), BF)], (place, one, more, two), 0)
            other = over_rank(q)
            (out,) = call(
                lambda *r: last_kernel(source, *r),
                [S((half, c), BF)],
                (place, q, other, upper, y),
                field_flops // 3,
                [pltpu.VMEM((c, 4 * k), BF)],
            )
            return out
        there = over_rank(s)
        gram = lower_gram if flipped else upper_gram
        factor, after = (lower, upper) if flipped else (upper, lower)
        packed, q = call(next_kernel, [p_shape, s_shape], (place, *pieces, gram, s, there), 2 * wide * wide * c)
        other = over_rank(q)
        (summed,) = call(
            lambda *r: again_kernel(source, *r), [p_shape], (place, packed, other, gram, s, there), 2 * wide * wide * c
        )
        (q,) = call(lambda *r: pick_kernel(source, *r), [s_shape], (place, q, other), 0)
        (y,) = call(lambda *r: field_kernel(not flipped, *r), [y_shape], (place, q, factor, y, leaves), field_flops // 2)
        if step + 2 < applies:
            (s,) = call(project_kernel, [s_shape], (place, y, after), field_flops // 2)


def solution(mesh):
    rows = P(("parts", "rows", "cols"), None)
    split = P(("parts", "rows", "cols"), "rank")
    every = ("parts", "rows", "cols", "rank")
    in_specs = (rows,) + (split,) * 6 + (P(every, None, None),)

    return jax.shard_map(local, mesh=mesh, in_specs=in_specs, out_specs=P(every, None), check_vma=False)
```

```python
import jax
import jax.numpy as jnp
from jax import lax
from jax.experimental import pallas as pl
from jax.experimental.pallas import tpu as pltpu
from jax.sharding import PartitionSpec as P


PASSES = 2
LEVELS = 3
BLOCKS = tuple((i, j) for i in range(LEVELS) for j in range(i + 1))
BF = jnp.bfloat16
F32 = jnp.float32
VMEM_BYTES = 12 * 2**20


def mm(a, b, ca, cb):
    return lax.dot_general(a, b, (((ca,), (cb,)), ((), ())), preferred_element_type=F32)


def call(kernel, outs, args, flops, scratch=(), far=0, keep=True):
    vm = pl.BlockSpec(memory_space=pltpu.VMEM)
    hbm = pl.BlockSpec(memory_space=pltpu.HBM)
    near, distant = args[: len(args) - far], args[len(args) - far :]
    moved = sum(a.size * a.dtype.itemsize for a in args[1:]) + sum(o.size * o.dtype.itemsize for o in outs)
    return pl.pallas_call(
        kernel,
        out_shape=outs,
        in_specs=[pl.BlockSpec(memory_space=pltpu.SMEM)] + [vm] * (len(args) - 1 - far) + [hbm] * far,
        out_specs=[vm if keep else hbm] * len(outs),
        scratch_shapes=list(scratch),
        cost_estimate=pl.CostEstimate(flops=flops, bytes_accessed=moved, transcendentals=0),
        compiler_params=pltpu.CompilerParams(vmem_limit_bytes=VMEM_BYTES),
    )(*near, *(pltpu.with_memory_space_constraint(a, pltpu.HBM) for a in distant))


def at(start, size):
    return pl.ds(pl.multiple_of(start, size), size)


def first_kernel(place, *refs):
    sources, out, buffers, sems = refs[: LEVELS + 1], refs[LEVELS + 1], refs[LEVELS + 2 : -1], refs[-1]
    copies = [pltpu.make_async_copy(a, b, sems.at[i]) for i, (a, b) in enumerate(zip(sources, buffers))]
    for copy in copies:
        copy.start()
    copies[0].wait()
    zt = buffers[0][...].T
    c = zt.shape[0]
    for level in range(LEVELS):
        copies[1 + level].wait()
        out[level * c : (level + 1) * c, :] = mm(zt, buffers[1 + level][...], 1, 0).astype(BF)


def pack_kernel(place, *refs):
    sources, out = refs[:LEVELS], refs[LEVELS]
    half = out.shape[0] // LEVELS
    for i, a in enumerate(sources):
        out[i * half : (i + 1) * half, :] = a[at((1 - place[0]) * half, half), :]


def beside_kernel(place, left, right, out):
    k = left.shape[1]
    out[:, :k] = left[...]
    out[:, k:] = right[...]


def join_kernel(place, own, other, out):
    k = own.shape[1]
    me = place[0]
    out[:, at(me * k, k)] = own[...]
    out[:, at((1 - me) * k, k)] = other[...]


def gram_kernel(place, other, *refs):
    own, (full, gram) = refs[:LEVELS], refs[LEVELS:]
    half, k = other.shape[0] // LEVELS, other.shape[1]
    me = place[0]
    for level in range(LEVELS):
        full[:, at((2 * level + me) * k, k)] = own[level][at(me * half, half), :]
        full[:, at((2 * level + 1 - me) * k, k)] = other[level * half : (level + 1) * half, :]
    wide = 2 * k
    for n, (i, j) in enumerate(BLOCKS):
        if j == 0:
            left = full[:, i * wide : (i + 1) * wide].T
        gram[n * wide : (n + 1) * wide, :] = mm(left, full[:, j * wide : (j + 1) * wide], 1, 0).astype(BF)


def whole_kernel(place, mine, other, out):
    k = mine.shape[1]
    for n, (i, j) in enumerate(BLOCKS):
        block = add(mine[n * k : (n + 1) * k, :], other[n * k : (n + 1) * k, :])
        out[i * k : (i + 1) * k, j * k : (j + 1) * k] = block
        if j < i:
            out[j * k : (j + 1) * k, i * k : (i + 1) * k] = block.T


def join_siblings(one, more, two, three, joined):
    k = one.shape[1]
    joined[:, :k] = add(one[...], more[...])
    joined[:, k : 2 * k] = two[...]
    joined[:, 2 * k :] = three[...]


def base_kernel(place, three, gram, here, there, out):
    c, k = three.shape
    for level in range(LEVELS):
        cols = slice(level * k, (level + 1) * k)
        total = here[:, cols].astype(F32) + there[:, cols].astype(F32)
        out[level * c : (level + 1) * c, :] = total + mm(three[...], gram[-k:, cols], 1, 0)


def next_kernel(place, one, more, two, three, gram, base, out, joined):
    join_siblings(one, more, two, three, joined)
    c, k = one.shape
    for level in range(LEVELS):
        rows, cols = slice(level * c, (level + 1) * c), slice(level * k, (level + 1) * k)
        out[rows, :] = (base[rows, :] + mm(joined[:, : 2 * k], gram[: 2 * k, cols], 1, 0)).astype(BF)


def again_kernel(holder, place, early, other, gram, here, there, out):
    @pl.when(place[0] == holder)
    def _():
        out[...] = early[...]

    @pl.when(place[0] != holder)
    def _():
        c, k = out.shape[0] // LEVELS, out.shape[1]
        for level in range(LEVELS):
            cols = slice(level * k, (level + 1) * k)
            total = here[:, cols].astype(F32) + there[:, cols].astype(F32) + mm(other[...], gram[:, cols], 1, 0)
            out[level * c : (level + 1) * c, :] = total.astype(BF)


def pick_kernel(holder, place, mine, other, out):
    @pl.when(place[0] == holder)
    def _():
        out[...] = mine[...]

    @pl.when(place[0] != holder)
    def _():
        out[...] = other[...]


def sum_kernel(source, place, summed, received, relayed, out):
    n = out.shape[0]

    @pl.when(place[0] == source)
    def _():
        out[...] = add(summed[:n, :], relayed[:n, :])

    @pl.when(place[0] != source)
    def _():
        out[...] = add(summed[:n, :], received[:n, :])


def leaf_terms(z, leaves, flipped, out):
    size = leaves.shape[1]
    for q in range(leaves.shape[0]):
        rows = slice(q * size, (q + 1) * size)
        out[rows, :] = mm(leaves[q], z[rows, :], 0 if flipped else 1, 0)


def start_kernel(place, z, leaves, after, y, s):
    half = y.shape[0]
    leaf_terms(z[at(place[0] * half, half), :], leaves, True, y)
    s[...] = mm(y[...].astype(BF).T, after[...], 1, 0).astype(BF)


def project_kernel(place, y, after, s):
    s[...] = mm(y[...].astype(BF).T, after[...], 1, 0).astype(BF)


def field_kernel(flipped, place, q, factor, was, leaves, y):
    z = (mm(factor[...], q[...], 1, 1) + was[...]).astype(BF)
    leaf_terms(z, leaves, flipped, y)


def siblings_kernel(place, one, more, two, out):
    k = one.shape[1]
    out[:, :k] = add(one[...], more[...])
    out[:, k:] = two[...]


def most_kernel(holder, place, three, other, factor, was, y, joined):
    pick_kernel(holder, place, three, other, joined)
    y[...] = mm(factor[:, -joined.shape[1] :], joined[...], 1, 1) + was[...]


def last_kernel(holder, place, mine, other, factor, was, out, joined, rows, sems):
    pick_kernel(holder, place, mine, other, joined)
    parts = sems.shape[0]
    size = rows.shape[0] // parts
    copies = []
    for i in range(parts):
        part = pl.ds(i * size, size)
        rows[part, :] = (mm(factor[part, : joined.shape[1]], joined[...], 1, 1) + was[part, :]).astype(BF)
        copies.append(pltpu.make_async_copy(rows.at[part, :], out.at[part, :], sems.at[i]))
        copies[-1].start()
    for copy in copies:
        copy.wait()


def one_way(value, mask, source):
    chips = lax.axis_size(("rows", "cols"))
    away = [(2 * p + source, 2 * (p ^ mask) + 1 - source) for p in range(chips)]
    home = [(2 * p + 1 - source, 2 * p + source) for p in range(chips)]
    return lax.ppermute(value, ("rows", "cols", "rank"), away + home)


def over_rank(value):
    return lax.ppermute(value, "rank", [(0, 1), (1, 0)])


def add(a, b):
    return (a.astype(F32) + b.astype(F32)).astype(BF)


def gathered(place, packed, summed, source):
    chips = lax.axis_size(("rows", "cols"))
    stride = 1
    while stride < chips // 2**LEVELS:
        received = one_way(packed, stride, source)
        relayed = over_rank(received)
        packed = add(summed, received)
        shape = jax.ShapeDtypeStruct(packed.shape, BF)
        (summed,) = call(
            lambda *r, source=source: sum_kernel(source, *r), [shape], (place, summed, received, relayed), 0
        )
        source, stride = 1 - source, 2 * stride
    return packed, summed, source, stride


def add_kernel(place, one, two, out):
    out[...] = add(one[...], two[...])


def siblings_of(place, packed, summed, source, stride, received=None):
    c = packed.shape[0] // LEVELS
    if received is None:
        received = one_way(packed[:c], stride, source)
        below = one_way(packed[c : 2 * c], stride, source)
    else:
        received, below = received[:c], received[c:]
    three = one_way(summed[2 * c :], stride, 1 - source)
    both = add(summed[:c], received)
    one = one_way(both, 6 * stride, 1 - source)
    more = one_way(both, 4 * stride, 1 - source)
    shape = jax.ShapeDtypeStruct(below.shape, BF)
    (under,) = call(add_kernel, [shape], (place, summed[c : 2 * c], below), 0)
    two = one_way(under, 2 * stride, 1 - source)
    return one, more, two, three


def local(probes, basis_one, basis_two, basis_three, coeff_one, coeff_two, coeff_three, leaves):
    place = lax.axis_index("rank").reshape(1)
    n, c = probes.shape
    half = n // 2
    k = basis_one.shape[1]
    wide = 2 * k * LEVELS
    S = jax.ShapeDtypeStruct
    p_shape, y_shape, s_shape = S((LEVELS * c, 2 * k), BF), S((half, c), F32), S((c, wide), BF)
    sems = pltpu.SemaphoreType.DMA
    uppers = (basis_one, basis_two, basis_three)
    lowers = (coeff_one, coeff_two, coeff_three)

    def prepared(factors):
        (sent,) = call(pack_kernel, [S((LEVELS * half, k), BF)], (place, *factors), 0)
        other = over_rank(sent)
        full, gram = call(
            gram_kernel,
            [S((half, wide), BF), S((len(BLOCKS) * 2 * k, 2 * k), BF)],
            (place, other, *factors),
            half * wide * wide * 3 // 2,
        )
        other = over_rank(gram)
        (gram,) = call(whole_kernel, [S((wide, wide), BF)], (place, gram, other), 0)
        return full, gram

    buffers = [pltpu.VMEM(a.shape, BF) for a in (probes, *uppers)]
    (own,) = call(
        first_kernel,
        [S((LEVELS * c, k), BF)],
        (place, probes, *uppers),
        2 * n * LEVELS * k * c,
        [*buffers, sems((LEVELS + 1,))],
        LEVELS + 1,
    )
    other = over_rank(own)
    (summed,) = call(join_kernel, [p_shape], (place, own, other), 0)
    packed, received = summed, None
    if lax.axis_size(("rows", "cols")) == 2**LEVELS:
        left = one_way(own[: 2 * c], 1, 0)
        right = one_way(other[: 2 * c], 1, 0)
        (received,) = call(beside_kernel, [S((2 * c, 2 * k), BF)], (place, left, right), 0)
    lower, lower_gram = prepared(lowers)
    upper, upper_gram = prepared(uppers)
    field_flops = 4 * half * wide * c
    y, s = call(start_kernel, [y_shape, s_shape], (place, probes, leaves, lower), field_flops // 2)
    applies = 2 * PASSES
    source = 0
    for step in range(applies):
        flipped = step % 2 == 0
        packed, summed, source, stride = gathered(place, packed, summed, source)
        pieces = siblings_of(place, packed, summed, source, stride, received)
        received = None
        if step + 1 == applies:
            one, more, two, three = pieces
            other = over_rank(three)
            (y,) = call(
                lambda *r: most_kernel(source, *r),
                [y_shape],
                (place, three, other, upper, y),
                field_flops // 6,
                [pltpu.VMEM((c, 2 * k), BF)],
            )
            (q,) = call(siblings_kernel, [S((c, 4 * k), BF)], (place, one, more, two), 0)
            other = over_rank(q)
            (out,) = call(
                lambda *r: last_kernel(source, *r),
                [S((half, c), BF)],
                (place, q, other, upper, y),
                field_flops // 3,
                [pltpu.VMEM((c, 4 * k), BF), pltpu.VMEM((half, c), BF), sems((2,))],
                keep=False,
            )
            return out
        there = over_rank(s)
        gram = lower_gram if flipped else upper_gram
        factor, after = (lower, upper) if flipped else (upper, lower)
        (base,) = call(base_kernel, [S(p_shape.shape, F32)], (place, pieces[3], gram, s, there), wide * wide * c)
        packed, q = call(next_kernel, [p_shape, s_shape], (place, *pieces, gram, base), 2 * wide * wide * c)
        other = over_rank(q)
        (summed,) = call(
            lambda *r: again_kernel(source, *r), [p_shape], (place, packed, other, gram, s, there), 2 * wide * wide * c
        )
        (q,) = call(lambda *r: pick_kernel(source, *r), [s_shape], (place, q, other), 0)
        (y,) = call(lambda *r: field_kernel(not flipped, *r), [y_shape], (place, q, factor, y, leaves), field_flops // 2)
        if step + 2 < applies:
            (s,) = call(project_kernel, [s_shape], (place, y, after), field_flops // 2)


def solution(mesh):
    rows = P(("parts", "rows", "cols"), None)
    split = P(("parts", "rows", "cols"), "rank")
    every = ("parts", "rows", "cols", "rank")
    in_specs = (rows,) + (split,) * 6 + (P(every, None, None),)

    return jax.shard_map(local, mesh=mesh, in_specs=in_specs, out_specs=P(every, None), check_vma=False)
```

```python
import jax
import jax.numpy as jnp
from jax import lax
from jax.experimental import pallas as pl
from jax.experimental.pallas import tpu as pltpu
from jax.sharding import PartitionSpec as P


PASSES = 2
LEVELS = 3
BLOCKS = tuple((i, j) for i in range(LEVELS) for j in range(i + 1))
BF = jnp.bfloat16
F32 = jnp.float32
VMEM_BYTES = 12 * 2**20


def mm(a, b, ca, cb):
    return lax.dot_general(a, b, (((ca,), (cb,)), ((), ())), preferred_element_type=F32)


def call(kernel, outs, args, flops, scratch=(), far=0, keep=True):
    vm = pl.BlockSpec(memory_space=pltpu.VMEM)
    hbm = pl.BlockSpec(memory_space=pltpu.HBM)
    near, distant = args[: len(args) - far], args[len(args) - far :]
    moved = sum(a.size * a.dtype.itemsize for a in args[1:]) + sum(o.size * o.dtype.itemsize for o in outs)
    return pl.pallas_call(
        kernel,
        out_shape=outs,
        in_specs=[pl.BlockSpec(memory_space=pltpu.SMEM)] + [vm] * (len(args) - 1 - far) + [hbm] * far,
        out_specs=[vm if keep else hbm] * len(outs),
        scratch_shapes=list(scratch),
        cost_estimate=pl.CostEstimate(flops=flops, bytes_accessed=moved, transcendentals=0),
        compiler_params=pltpu.CompilerParams(vmem_limit_bytes=VMEM_BYTES),
    )(*near, *(pltpu.with_memory_space_constraint(a, pltpu.HBM) for a in distant))


def at(start, size):
    return pl.ds(pl.multiple_of(start, size), size)


def first_kernel(place, *refs):
    sources, out, buffers, sems = refs[: LEVELS + 1], refs[LEVELS + 1], refs[LEVELS + 2 : -1], refs[-1]
    copies = [pltpu.make_async_copy(a, b, sems.at[i]) for i, (a, b) in enumerate(zip(sources, buffers))]
    for copy in copies:
        copy.start()
    copies[0].wait()
    zt = buffers[0][...].T
    c = zt.shape[0]
    for level in range(LEVELS):
        copies[1 + level].wait()
        out[level * c : (level + 1) * c, :] = mm(zt, buffers[1 + level][...], 1, 0).astype(BF)


def pack_kernel(place, *refs):
    sources, out = refs[:LEVELS], refs[LEVELS]
    half = out.shape[0] // LEVELS
    for i, a in enumerate(sources):
        out[i * half : (i + 1) * half, :] = a[at((1 - place[0]) * half, half), :]


def beside_kernel(place, left, right, out):
    k = left.shape[1]
    out[:, :k] = left[...]
    out[:, k:] = right[...]


def join_kernel(place, own, other, out):
    k = own.shape[1]
    me = place[0]
    out[:, at(me * k, k)] = own[...]
    out[:, at((1 - me) * k, k)] = other[...]


def gram_kernel(place, other, *refs):
    own, (full, gram) = refs[:LEVELS], refs[LEVELS:]
    half, k = other.shape[0] // LEVELS, other.shape[1]
    me = place[0]
    for level in range(LEVELS):
        full[:, at((2 * level + me) * k, k)] = own[level][at(me * half, half), :]
        full[:, at((2 * level + 1 - me) * k, k)] = other[level * half : (level + 1) * half, :]
    wide = 2 * k
    for n, (i, j) in enumerate(BLOCKS):
        if j == 0:
            left = full[:, i * wide : (i + 1) * wide].T
        gram[n * wide : (n + 1) * wide, :] = mm(left, full[:, j * wide : (j + 1) * wide], 1, 0).astype(BF)


def whole_kernel(place, mine, other, out):
    k = mine.shape[1]
    for n, (i, j) in enumerate(BLOCKS):
        block = add(mine[n * k : (n + 1) * k, :], other[n * k : (n + 1) * k, :])
        out[i * k : (i + 1) * k, j * k : (j + 1) * k] = block
        if j < i:
            out[j * k : (j + 1) * k, i * k : (i + 1) * k] = block.T


def join_siblings(one, more, two, three, joined):
    k = one.shape[1]
    joined[:, :k] = add(one[...], more[...])
    joined[:, k : 2 * k] = two[...]
    joined[:, 2 * k :] = three[...]


def base_kernel(place, three, gram, here, there, out):
    c, k = three.shape
    for level in range(LEVELS):
        cols = slice(level * k, (level + 1) * k)
        total = here[:, cols].astype(F32) + there[:, cols].astype(F32)
        out[level * c : (level + 1) * c, :] = total + mm(three[...], gram[-k:, cols], 1, 0)


def next_kernel(place, one, more, two, three, gram, base, out, joined):
    join_siblings(one, more, two, three, joined)
    c, k = one.shape
    for level in range(LEVELS):
        rows, cols = slice(level * c, (level + 1) * c), slice(level * k, (level + 1) * k)
        out[rows, :] = (base[rows, :] + mm(joined[:, : 2 * k], gram[: 2 * k, cols], 1, 0)).astype(BF)


def again_kernel(holder, place, early, other, gram, here, there, out):
    @pl.when(place[0] == holder)
    def _():
        out[...] = early[...]

    @pl.when(place[0] != holder)
    def _():
        c, k = out.shape[0] // LEVELS, out.shape[1]
        for level in range(LEVELS):
            cols = slice(level * k, (level + 1) * k)
            total = here[:, cols].astype(F32) + there[:, cols].astype(F32) + mm(other[...], gram[:, cols], 1, 0)
            out[level * c : (level + 1) * c, :] = total.astype(BF)


def pick_kernel(holder, place, mine, other, out):
    @pl.when(place[0] == holder)
    def _():
        out[...] = mine[...]

    @pl.when(place[0] != holder)
    def _():
        out[...] = other[...]


def sum_kernel(source, place, summed, received, relayed, out):
    n = out.shape[0]

    @pl.when(place[0] == source)
    def _():
        out[...] = add(summed[:n, :], relayed[:n, :])

    @pl.when(place[0] != source)
    def _():
        out[...] = add(summed[:n, :], received[:n, :])


def leaf_terms(z, leaves, flipped, out):
    size = leaves.shape[1]
    for q in range(leaves.shape[0]):
        rows = slice(q * size, (q + 1) * size)
        out[rows, :] = mm(leaves[q], z[rows, :], 0 if flipped else 1, 0)


def start_kernel(place, z, leaves, after, y, s):
    half = y.shape[0]
    leaf_terms(z[at(place[0] * half, half), :], leaves, True, y)
    s[...] = mm(y[...].astype(BF).T, after[...], 1, 0).astype(BF)


def project_kernel(place, y, after, s):
    s[...] = mm(y[...].astype(BF).T, after[...], 1, 0).astype(BF)


def field_kernel(flipped, place, q, factor, was, leaves, y):
    z = (mm(factor[...], q[...], 1, 1) + was[...]).astype(BF)
    leaf_terms(z, leaves, flipped, y)


def siblings_kernel(place, one, more, two, out):
    k = one.shape[1]
    out[:, :k] = add(one[...], more[...])
    out[:, k:] = two[...]


def most_kernel(holder, place, three, other, factor, was, y, joined):
    pick_kernel(holder, place, three, other, joined)
    y[...] = mm(factor[:, -joined.shape[1] :], joined[...], 1, 1) + was[...]


def last_kernel(holder, place, mine, other, factor, was, out, joined, rows, sems):
    pick_kernel(holder, place, mine, other, joined)
    parts = sems.shape[0]
    size = rows.shape[0] // parts
    copies = []
    for i in range(parts):
        part = pl.ds(i * size, size)
        rows[part, :] = (mm(factor[part, : joined.shape[1]], joined[...], 1, 1) + was[part, :]).astype(BF)
        copies.append(pltpu.make_async_copy(rows.at[part, :], out.at[part, :], sems.at[i]))
        copies[-1].start()
    for copy in copies:
        copy.wait()


def one_way(value, mask, source):
    chips = lax.axis_size(("rows", "cols"))
    away = [(2 * p + source, 2 * (p ^ mask) + 1 - source) for p in range(chips)]
    home = [(2 * p + 1 - source, 2 * p + source) for p in range(chips)]
    return lax.ppermute(value, ("rows", "cols", "rank"), away + home)


def over_rank(value):
    return lax.ppermute(value, "rank", [(0, 1), (1, 0)])


def add(a, b):
    return (a.astype(F32) + b.astype(F32)).astype(BF)


def gathered(place, packed, summed, source):
    chips = lax.axis_size(("rows", "cols"))
    stride = 1
    while stride < chips // 2**LEVELS:
        received = one_way(packed, stride, source)
        relayed = over_rank(received)
        packed = add(summed, received)
        shape = jax.ShapeDtypeStruct(packed.shape, BF)
        (summed,) = call(
            lambda *r, source=source: sum_kernel(source, *r), [shape], (place, summed, received, relayed), 0
        )
        source, stride = 1 - source, 2 * stride
    return packed, summed, source, stride


def add_kernel(place, one, two, out):
    out[...] = add(one[...], two[...])


def siblings_of(place, packed, summed, source, stride, received=None):
    c = packed.shape[0] // LEVELS
    if received is None:
        received = one_way(packed[:c], stride, source)
    below = one_way(packed[c : 2 * c], stride, source)
    three = one_way(summed[2 * c :], stride, 1 - source)
    both = add(summed[:c], received)
    one = one_way(both, 6 * stride, 1 - source)
    more = one_way(both, 4 * stride, 1 - source)
    shape = jax.ShapeDtypeStruct(below.shape, BF)
    (under,) = call(add_kernel, [shape], (place, summed[c : 2 * c], below), 0)
    two = one_way(under, 2 * stride, 1 - source)
    return one, more, two, three


def local(probes, basis_one, basis_two, basis_three, coeff_one, coeff_two, coeff_three, leaves):
    place = lax.axis_index("rank").reshape(1)
    n, c = probes.shape
    half = n // 2
    k = basis_one.shape[1]
    wide = 2 * k * LEVELS
    S = jax.ShapeDtypeStruct
    p_shape, y_shape, s_shape = S((LEVELS * c, 2 * k), BF), S((half, c), F32), S((c, wide), BF)
    sems = pltpu.SemaphoreType.DMA
    uppers = (basis_one, basis_two, basis_three)
    lowers = (coeff_one, coeff_two, coeff_three)

    def prepared(factors):
        (sent,) = call(pack_kernel, [S((LEVELS * half, k), BF)], (place, *factors), 0)
        other = over_rank(sent)
        full, gram = call(
            gram_kernel,
            [S((half, wide), BF), S((len(BLOCKS) * 2 * k, 2 * k), BF)],
            (place, other, *factors),
            half * wide * wide * 3 // 2,
        )
        other = over_rank(gram)
        (gram,) = call(whole_kernel, [S((wide, wide), BF)], (place, gram, other), 0)
        return full, gram

    buffers = [pltpu.VMEM(a.shape, BF) for a in (probes, *uppers)]
    (own,) = call(
        first_kernel,
        [S((LEVELS * c, k), BF)],
        (place, probes, *uppers),
        2 * n * LEVELS * k * c,
        [*buffers, sems((LEVELS + 1,))],
        LEVELS + 1,
    )
    other = over_rank(own)
    (summed,) = call(join_kernel, [p_shape], (place, own, other), 0)
    packed, received = summed, None
    if lax.axis_size(("rows", "cols")) == 2**LEVELS:
        left = one_way(own[:c], 1, 0)
        right = one_way(other[:c], 1, 0)
        (received,) = call(beside_kernel, [S((c, 2 * k), BF)], (place, left, right), 0)
    lower, lower_gram = prepared(lowers)
    upper, upper_gram = prepared(uppers)
    field_flops = 4 * half * wide * c
    y, s = call(start_kernel, [y_shape, s_shape], (place, probes, leaves, lower), field_flops // 2)
    applies = 2 * PASSES
    source = 0
    for step in range(applies):
        flipped = step % 2 == 0
        packed, summed, source, stride = gathered(place, packed, summed, source)
        pieces = siblings_of(place, packed, summed, source, stride, received)
        received = None
        if step + 1 == applies:
            one, more, two, three = pieces
            other = over_rank(three)
            (y,) = call(
                lambda *r: most_kernel(source, *r),
                [y_shape],
                (place, three, other, upper, y),
                field_flops // 6,
                [pltpu.VMEM((c, 2 * k), BF)],
            )
            (q,) = call(siblings_kernel, [S((c, 4 * k), BF)], (place, one, more, two), 0)
            other = over_rank(q)
            (out,) = call(
                lambda *r: last_kernel(source, *r),
                [S((half, c), BF)],
                (place, q, other, upper, y),
                field_flops // 3,
                [pltpu.VMEM((c, 4 * k), BF), pltpu.VMEM((half, c), BF), sems((2,))],
                keep=False,
            )
            return out
        there = over_rank(s)
        gram = lower_gram if flipped else upper_gram
        factor, after = (lower, upper) if flipped else (upper, lower)
        (base,) = call(base_kernel, [S(p_shape.shape, F32)], (place, pieces[3], gram, s, there), wide * wide * c)
        packed, q = call(next_kernel, [p_shape, s_shape], (place, *pieces, gram, base), 2 * wide * wide * c)
        other = over_rank(q)
        (summed,) = call(
            lambda *r: again_kernel(source, *r), [p_shape], (place, packed, other, gram, s, there), 2 * wide * wide * c
        )
        (q,) = call(lambda *r: pick_kernel(source, *r), [s_shape], (place, q, other), 0)
        (y,) = call(lambda *r: field_kernel(not flipped, *r), [y_shape], (place, q, factor, y, leaves), field_flops // 2)
        if step + 2 < applies:
            (s,) = call(project_kernel, [s_shape], (place, y, after), field_flops // 2)


def solution(mesh):
    rows = P(("parts", "rows", "cols"), None)
    split = P(("parts", "rows", "cols"), "rank")
    every = ("parts", "rows", "cols", "rank")
    in_specs = (rows,) + (split,) * 6 + (P(every, None, None),)

    return jax.shard_map(local, mesh=mesh, in_specs=in_specs, out_specs=P(every, None), check_vma=False)
```
